128 devices in a mesh: bx: 32 (over x, z, core), by: 2 (over y_hi), col: 2 (over y_lo).
Axes of the slice: x: 4, y: 4 (y_hi: 2, y_lo: 2; y = y_hi * 2 + y_lo), z: 4, core: 2. Of those that a mesh axis runs over, the one named last changes fastest.
Arguments:
- multipoles: bfloat16 [2, 152, 32, 1024], P(None, 'col', 'bx', 'by'), may hold values from -6 to 6
- kernel: bfloat16 [2, 32, 32, 17, 152, 152], P(None, 'bx', 'by', None, 'col'), may hold values from -0.5 to 0.5
Outputs:
- locals_out: float32 [2, 152, 32, 1024], P(None, 'col', 'bx', 'by')
The draws below stay inside these ranges and needn't reach their ends.
All inputs are finite; a program needn't handle non-finite values.
Results may differ from the reference program's by a relative error of at most 0.0029.
Values may be sent and summed in bfloat16 or wider, within the bound.
No kernel may reach another device: no remote copies, remote signals or barrier semaphores. Data moves between devices by JAX's collectives and lax.ppermute only.
A program may use at most 128 MiB of HBM per device.

```python
import jax
import jax.numpy as jnp
from jax import lax

NB = 32
C = 152
RHS = 2
KZ = 17


def block_levels(key, dims, split, low, high):
    def one(axis_at, shards_of):
        draws = jax.random.uniform(jax.random.fold_in(jax.random.fold_in(key, 6), axis_at), (shards_of,), jnp.float32, low / len(split), high / len(split))
        return jnp.repeat(jnp.exp(draws), dims[axis_at] // shards_of).reshape((-1,) + (1,) * (len(dims) - axis_at - 1))

    level = one(*split[0])
    for cut in split[1:]:
        level = level * one(*cut)
    return level


def normal_values(own_key, extent, scale, most, split=(), kind=jnp.bfloat16):
    array = scale * jax.random.normal(own_key, extent, jnp.float32)
    if split:
        array = array * block_levels(own_key, extent, split, -0.22, 0.18)
    return jnp.clip(array, -most, most).astype(kind)


def setup_inputs(seed: int = 0) -> dict:
    key_of = jax.random.split(jax.random.key(seed), 3)
    multipoles = normal_values(key_of[0], (RHS, C, NB, NB * NB), 1.0, 6.0, ((1, 2), (2, 32), (3, 2)))
    kernel = normal_values(key_of[1], (2, NB, NB, KZ, C, C), C ** -0.5, 0.5, ((1, 32), (2, 2), (4, 2)))
    return {"multipoles": multipoles, "kernel": kernel}


def reference(multipoles, kernel):
    field_grid = multipoles.astype(jnp.float32).reshape(RHS, C, NB, NB, NB)
    waves = jnp.fft.rfftn(field_grid, axes=(2, 3, 4))
    spec_re = jnp.real(waves).astype(jnp.bfloat16)
    spec_im = jnp.imag(waves).astype(jnp.bfloat16)

    def per_plane(plane_index):
        kernel_plane = lax.dynamic_index_in_dim(kernel, plane_index, 1, keepdims=False).astype(jnp.float32)
        panel_re = lax.dynamic_index_in_dim(spec_re, plane_index, 2, keepdims=False).astype(jnp.float32)
        panel_im = lax.dynamic_index_in_dim(spec_im, plane_index, 2, keepdims=False).astype(jnp.float32)
        pattern = "bkij,rjbk->ribk"
        out_re = jnp.einsum(pattern, kernel_plane[0], panel_re) - jnp.einsum(pattern, kernel_plane[1], panel_im)
        out_im = jnp.einsum(pattern, kernel_plane[0], panel_im) + jnp.einsum(pattern, kernel_plane[1], panel_re)
        return out_re, out_im

    local_re, local_im = lax.map(per_plane, jnp.arange(NB, dtype=jnp.int32))
    local_re = jnp.moveaxis(local_re, 0, 2)
    local_im = jnp.moveaxis(local_im, 0, 2)
    result = jnp.fft.irfftn(lax.complex(local_re, local_im), s=(NB, NB, NB), axes=(2, 3, 4))
    return result.astype(jnp.float32).reshape(RHS, C, NB, NB * NB)
```

```python
import functools
import math

import jax
import jax.numpy as jnp
import numpy as np
from jax import lax
from jax.experimental import pallas as pl
from jax.experimental.pallas import tpu as pltpu
from jax.sharding import PartitionSpec as P

NB = 32
KZ = 17
RHS = 2
HALF = 38
SPARE = 19
F32 = jnp.float32
BF16 = jnp.bfloat16


def to_bf16(values):
    return np.asarray(values, np.float32).astype(jnp.bfloat16)


def table_scale():
    level = np.cos(2 * np.pi * np.arange(8) / 32)
    weight = np.array([2.0] + [4.0] * 7)
    scales = np.linspace(1.0, 2.0, 20001)[:-1]
    scaled = scales[:, None] * level[None, :]
    error = to_bf16(scaled).astype(np.float64) / scales[:, None] - level[None, :]
    return float(scales[np.argmin((weight * error**2).sum(1))])


SCALE = table_scale()


def split(table):
    high = to_bf16(SCALE * table)
    return high, to_bf16(SCALE * table - high.astype(np.float64))


def tables_z():
    kz = np.arange(KZ)[:, None]
    z = np.arange(NB)[None, :]
    angle = 2 * np.pi * ((kz * z) % NB) / NB
    eye = np.eye(16)
    cos = np.einsum("kz,ab->kabz", np.cos(angle), eye).reshape(KZ * 16, 16 * NB)
    sin = np.einsum("kz,ab->kabz", -np.sin(angle), eye).reshape(KZ * 16, 16 * NB)
    return np.stack(split(cos)), np.stack(split(sin[:256]))


def table_line():
    k = np.arange(NB)
    angle = 2 * np.pi * ((k[:, None] * k[None, :]) % NB) / NB
    high, low = split(np.concatenate([np.cos(angle), np.sin(angle)]))
    return np.concatenate([high, low, high], 1)


def select_in():
    table = np.zeros((4, 128, 512), np.float32)
    c = np.arange(HALF)
    for half in range(2):
        for column in range(2):
            target = column * 76 + half * HALF + c
            table[half * 2 + column, c, target] = 1
            table[half * 2 + column, 64 + c, 256 + target] = 1
    return to_bf16(table)


def select_out():
    table = np.zeros((2, 256, 128), np.float32)
    c = np.arange(HALF)
    for half in range(2):
        table[half, half * HALF + c, c] = 1
        table[half, 128 + half * HALF + c, 64 + c] = 1
    return to_bf16(table)


def lane_index(rows):
    return lax.broadcasted_iota(jnp.int32, (rows, 128), 1)


def lanes_between(rows, low, high):
    lane = lane_index(rows) % 64
    return (lane >= low) & (lane < high)


def dot_nt(left, right):
    return lax.dot_general(left, right, (((1,), (1,)), ((), ())), preferred_element_type=F32)


def dot_tn(left, right):
    return lax.dot_general(left, right, (((0,), (0,)), ((), ())), preferred_element_type=F32)


def dot(left, right):
    return jnp.dot(left, right, preferred_element_type=F32)


def spread_last(last, rows):
    spare = lanes_between(rows, HALF, HALF + SPARE)
    first = jnp.where(spare, pltpu.roll(last, HALF, 1), 0.0)
    second = jnp.where(spare, pltpu.roll(last, HALF - SPARE, 1), 0.0)
    return first, second


def gather_last(first, second, rows):
    first = jnp.where(lanes_between(rows, 0, SPARE), pltpu.roll(first, 128 - HALF, 1), 0.0)
    second = jnp.where(
        lanes_between(rows, SPARE, HALF), pltpu.roll(second, 128 - HALF + SPARE, 1), 0.0
    )
    return first + second


def along_z_kernel(field_ref, cos_ref, sin_ref, out_ref):
    for group in range(4):
        field_re = field_ref[group, 64:192, :]
        field_im = field_ref[group, 0:128, :]
        waves = dot_nt(cos_ref[0], field_re) + dot_nt(cos_ref[1], field_re)
        first, second = spread_last(waves[256:272], 16)
        extra = jnp.concatenate([first, second, jnp.zeros((224, 128), F32)], 0)
        waves = waves[:256] + dot_nt(sin_ref[0], field_im) + dot_nt(sin_ref[1], field_im) + extra
        out_ref[:, group] = waves.reshape(16, 16, 128)


def line_waves(table, pair, sign):
    both = jnp.concatenate(pair, 1)
    high = both.astype(BF16)
    if both.dtype == BF16:
        stacked = jnp.concatenate([high, high], 0)
    else:
        low = (both - high.astype(F32)).astype(BF16)
        stacked = jnp.concatenate([high, high, low], 0)
    product = dot(table[:, : stacked.shape[0]], stacked)
    upper = lane_index(32) < 64
    result = []
    for lane in (0, 128):
        crossed = pltpu.roll(product[32:, lane : lane + 128], 64, 1)
        result.append(
            product[:32, lane : lane + 128] + jnp.where(upper, sign * crossed, -sign * crossed)
        )
    return result


def plane_kernel(sign, scale, copies, data_ref, table_ref, out_ref, middle_ref, end_ref):
    table = table_ref[...]
    for x in range(0, NB, 2):
        pair = [data_ref[2 * i : 2 * i + 2].reshape(32, 128) for i in (x, x + 1)]
        for i, rows in enumerate(line_waves(table, pair, sign)):
            middle_ref[(x + i) * 32 : (x + i + 1) * 32, :] = rows
    for y in range(0, NB, 2):
        pair = [middle_ref[pl.ds(i, 32, stride=32), :] for i in (y, y + 1)]
        for i, rows in enumerate(line_waves(table, pair, sign)):
            end_ref[pl.ds(y + i, 32, stride=32), :] = rows
    total = (end_ref[...] * scale).astype(BF16).reshape(64, 16, 128)
    for copy in range(copies):
        out_ref[:, copy] = total


def frequency_kernel(
    spec_ref, kernel_ref, select_ref, back_ref, out_ref, left_ref, right_ref, local_ref
):
    step = pl.program_id(0)

    @pl.when(step == 0)
    def _():
        total = jnp.zeros((512, 512), F32)
        last = jnp.zeros((32, 512), F32)
        for group in range(4):
            panel = spec_ref[:, :, group].reshape(512, 128)
            total += dot(panel, select_ref[group])
            closing = gather_last(panel[0:32].astype(F32), panel[32:64].astype(F32), 32)
            last += dot(closing.astype(BF16), select_ref[group])
        for kz in range(KZ):
            for rhs in range(RHS):
                row = (kz * RHS + rhs) * 16
                rows = total[row : row + 16] if kz < 16 else last[rhs * 16 : rhs * 16 + 16]
                for ref, lane in ((left_ref, 0), (right_ref, 128)):
                    re = rows[:, lane : lane + 128]
                    im = rows[:, 256 + lane : 384 + lane]
                    for slot, value in ((0, re), (2, im), (4, -im), (6, re)):
                        ref[pl.ds(kz * 8 + slot + rhs, 16, stride=8 * KZ), :] = value

    for kz in range(KZ):
        row = pl.multiple_of(step * (8 * KZ) + kz * 8, 8)
        panel = jnp.concatenate(
            [left_ref[pl.ds(row, 8), :], right_ref[pl.ds(row, 8), :]], 1
        ).astype(BF16)[:, :152]
        first = dot_nt(panel, kernel_ref[0, 0, 0, kz])
        second = dot_nt(panel, kernel_ref[1, 0, 0, kz])
        local_ref[pl.ds(row, 8), 0:76] = first + pltpu.roll(second, 4, 0)

    @pl.when(step == 15)
    def _():
        keep = lane_index(16) < 76
        for rhs in range(RHS):
            rows = []
            for kz in range(KZ):
                weight = 1.0 if kz in (0, 16) else 2.0
                parts = []
                for slot in (rhs, 2 + rhs):
                    part = local_ref[pl.ds(kz * 8 + slot, 16, stride=8 * KZ), :]
                    parts.append(jnp.where(keep, part * weight, 0.0))
                rows.append(jnp.concatenate(parts, 1).astype(BF16))
            rows = jnp.concatenate(rows, 0)
            for half in range(2):
                chunk = dot(rows, back_ref[half])
                first, second = spread_last(chunk[256:272], 16)
                extra = jnp.concatenate([first, second, jnp.zeros((224, 128), F32)], 0)
                chunk = chunk[:256] + extra
                out_ref[:, rhs * 2 + half] = chunk.astype(BF16).reshape(16, 16, 128)


def from_z_kernel(scale, data_ref, cos_ref, sin_ref, out_ref):
    for group in range(4):
        data = data_ref[:, group].reshape(256, 128)
        last = gather_last(data[0:16].astype(F32), data[16:32].astype(F32), 16)
        full = jnp.concatenate([data, last.astype(BF16)], 0)
        straight = dot_tn(full, cos_ref[0])
        crossed = dot_tn(data, sin_ref[0])
        total = (straight[0:HALF] + crossed[64 : 64 + HALF]) * scale
        half = group % 2
        out_ref[group // 2, half * HALF : half * HALF + HALF, :] = total


def vmem(count):
    return [pl.BlockSpec(memory_space=pltpu.VMEM)] * count


def along_z(field, cos, sin):
    return pl.pallas_call(
        along_z_kernel,
        out_shape=jax.ShapeDtypeStruct((16, 4, 16, 128), F32),
        in_specs=vmem(3),
        out_specs=pl.BlockSpec(memory_space=pltpu.VMEM),
        name="along_z",
    )(field, cos, sin)


def planes(data, table, sign, scale, copies, name):
    return pl.pallas_call(
        functools.partial(plane_kernel, sign, scale, copies),
        out_shape=jax.ShapeDtypeStruct((64, copies, 16, 128), BF16),
        in_specs=vmem(2),
        out_specs=pl.BlockSpec(memory_space=pltpu.VMEM),
        scratch_shapes=[pltpu.VMEM((1024, 128), F32), pltpu.VMEM((1024, 128), F32)],
        name=name,
    )(data, table)


def frequencies(spectrum, kernel, select, back):
    return pl.pallas_call(
        frequency_kernel,
        grid=(16,),
        out_shape=jax.ShapeDtypeStruct((16, 4, 16, 128), BF16),
        in_specs=[
            pl.BlockSpec((16, 2, 4, 16, 128), lambda i: (0, 0, 0, 0, 0)),
            pl.BlockSpec((2, 1, 1, KZ, 76, 152), lambda i: (0, 0, i, 0, 0, 0)),
            pl.BlockSpec((4, 128, 512), lambda i: (0, 0, 0)),
            pl.BlockSpec((2, 256, 128), lambda i: (0, 0, 0)),
        ],
        out_specs=pl.BlockSpec((16, 4, 16, 128), lambda i: (0, 0, 0, 0)),
        scratch_shapes=[
            pltpu.VMEM((16 * KZ * 8, 128), F32),
            pltpu.VMEM((16 * KZ * 8, 128), F32),
            pltpu.VMEM((16 * KZ * 8, 128), F32),
        ],
        name="frequencies",
    )(spectrum, kernel, select, back)


def from_z(data, cos, sin, scale):
    return pl.pallas_call(
        functools.partial(from_z_kernel, scale),
        out_shape=jax.ShapeDtypeStruct((2, 76, 512), F32),
        in_specs=vmem(3),
        out_specs=pl.BlockSpec(memory_space=pltpu.VMEM),
        name="from_z",
    )(data, cos, sin)


def exchange(chunks, axes):
    return lax.all_to_all(chunks, axes, 0, 0, tiled=True)


def on_device(multipoles, kernel):
    cos_z, sin_z = (jnp.asarray(t) for t in tables_z())
    table = jnp.asarray(table_line())
    near = ("bx", "by")
    field = jnp.pad(multipoles.reshape(4, HALF, 512), ((0, 0), (64, 192 - 64 - HALF), (0, 0)))
    waves = along_z(field, cos_z, sin_z).reshape(64, 16, 128)
    waves = exchange(waves, near)
    spectrum = planes(waves, table, 1.0, 1.0 / SCALE**3, 2, "to_waves")
    spectrum = exchange(spectrum.reshape(128, 16, 128), ("bx", "by", "col"))
    local = frequencies(
        spectrum.reshape(16, 2, 4, 16, 128),
        kernel,
        jnp.asarray(select_in()),
        jnp.asarray(select_out()),
    )
    local = exchange(local.reshape(64, 16, 128), near)
    back = planes(local, table, -1.0, 1.0 / (1024 * SCALE**2), 1, "from_waves")
    back = exchange(back.reshape(64, 16, 128), near)
    result = from_z(back.reshape(16, 4, 16, 128), cos_z, sin_z, 1.0 / (32 * SCALE))
    return result.reshape(multipoles.shape)


def solution(mesh):
    placed = (P(None, "col", "bx", "by"), P(None, "bx", "by", None, "col", None))
    return jax.shard_map(
        on_device, mesh=mesh, in_specs=placed, out_specs=P(None, "col", "bx", "by"), check_vma=False
    )
```

```python
import functools
import math

import jax
import jax.numpy as jnp
import numpy as np
from jax import lax
from jax.experimental import pallas as pl
from jax.experimental.pallas import tpu as pltpu
from jax.sharding import PartitionSpec as P

NB = 32
KZ = 17
RHS = 2
HALF = 38
SPARE = 19
F32 = jnp.float32
BF16 = jnp.bfloat16


def to_bf16(values):
    return np.asarray(values, np.float32).astype(jnp.bfloat16)


def table_scale():
    level = np.cos(2 * np.pi * np.arange(8) / 32)
    weight = np.array([2.0] + [4.0] * 7)
    scales = np.linspace(1.0, 2.0, 20001)[:-1]
    scaled = scales[:, None] * level[None, :]
    error = to_bf16(scaled).astype(np.float64) / scales[:, None] - level[None, :]
    return float(scales[np.argmin((weight * error**2).sum(1))])


SCALE = table_scale()


def split(table):
    high = to_bf16(SCALE * table)
    return high, to_bf16(SCALE * table - high.astype(np.float64))


def tables_z():
    kz = np.arange(KZ)[:, None]
    z = np.arange(NB)[None, :]
    angle = 2 * np.pi * ((kz * z) % NB) / NB
    eye = np.eye(8)
    cos = np.einsum("kz,ab->kabz", np.cos(angle), eye).reshape(KZ * 8, 8 * NB)
    sin = np.einsum("kz,ab->kabz", -np.sin(angle), eye).reshape(KZ * 8, 8 * NB)
    sin[128:] = 0
    cos_high, cos_low = split(cos)
    sin_high, sin_low = split(sin)
    ahead = np.concatenate([cos_high, cos_low, sin_high[:128], sin_low[:128]], 0)
    return ahead, np.concatenate([cos_high, sin_high], 1)


def table_line():
    k = np.arange(NB)
    angle = 2 * np.pi * ((k[:, None] * k[None, :]) % NB) / NB
    high, low = split(np.concatenate([np.cos(angle), np.sin(angle)]))
    return np.concatenate([high, low, high], 1)


def select_in():
    table = np.zeros((4, 128, 512), np.float32)
    c = np.arange(HALF)
    for half in range(2):
        for column in range(2):
            target = column * 76 + half * HALF + c
            table[half * 2 + column, c, target] = 1
            table[half * 2 + column, 64 + c, 256 + target] = 1
    return to_bf16(table)


def select_out():
    table = np.zeros((76, 16, 2, 128), np.float32)
    c = np.arange(HALF)
    for half in range(2):
        table[half * HALF + c, :, half, c] = 1
    return to_bf16(table.reshape(76 * 16, 256))


def lane_index(rows):
    return lax.broadcasted_iota(jnp.int32, (rows, 128), 1)


def lanes_between(rows, low, high):
    lane = lane_index(rows) % 64
    return (lane >= low) & (lane < high)


def dot_nt(left, right):
    return lax.dot_general(left, right, (((1,), (1,)), ((), ())), preferred_element_type=F32)


def dot_tn(left, right):
    return lax.dot_general(left, right, (((0,), (0,)), ((), ())), preferred_element_type=F32)


def dot(left, right):
    return jnp.dot(left, right, preferred_element_type=F32)


def spread_last(last, rows, base=0):
    spare = lanes_between(rows, HALF, HALF + SPARE)
    first = jnp.where(spare, pltpu.roll(last, (HALF - base) % 128, 1), 0.0)
    second = jnp.where(spare, pltpu.roll(last, (HALF - SPARE - base) % 128, 1), 0.0)
    return first, second


def gather_last(first, second, rows):
    first = jnp.where(lanes_between(rows, 0, SPARE), pltpu.roll(first, 128 - HALF, 1), 0.0)
    second = jnp.where(
        lanes_between(rows, SPARE, HALF), pltpu.roll(second, 128 - HALF + SPARE, 1), 0.0
    )
    return first + second


def along_z_kernel(field_ref, table_ref, out_ref, padded_ref):
    padded_ref[...] = jnp.zeros_like(padded_ref)
    for group in range(4):
        padded_ref[group * 64 : group * 64 + HALF, :] = field_ref[group]
    lower = lane_index(128) < 64
    spare = lanes_between(8, HALF, HALF + SPARE) & (lane_index(8) < 64)
    for block in range(2):
        product = dot_nt(table_ref[...], padded_ref[:, block * 256 : block * 256 + 256])
        cos = product[0:136] + product[136:272]
        sin = product[272:400] + product[400:528]
        for group in range(4):
            tile = slice(group // 2 * 128, group // 2 * 128 + 128)
            re, im, last = cos[:128, tile], sin[:, tile], cos[128:, tile]
            if group % 2 == 0:
                im = pltpu.roll(im, 64, 1)
            else:
                re = pltpu.roll(re, 64, 1)
            chunk = jnp.where(lower, re, im).reshape(16, 8, 128)
            first, second = spread_last(last, 8, group % 2 * 64)
            rows = slice(block * 8, block * 8 + 8)
            out_ref[:, group, rows, :] = chunk
            out_ref[0, group, rows, :] = chunk[0] + jnp.where(spare, first, 0.0)
            out_ref[1, group, rows, :] = chunk[1] + jnp.where(spare, second, 0.0)


def line_waves(table, pair, sign):
    both = jnp.concatenate(pair, 1)
    high = both.astype(BF16)
    if both.dtype == BF16:
        stacked = jnp.concatenate([high, high], 0)
    else:
        low = (both - high.astype(F32)).astype(BF16)
        stacked = jnp.concatenate([high, high, low], 0)
    product = dot(table[:, : stacked.shape[0]], stacked)
    upper = lane_index(32) < 64
    result = []
    for lane in (0, 128):
        crossed = pltpu.roll(product[32:, lane : lane + 128], 64, 1)
        result.append(
            product[:32, lane : lane + 128] + jnp.where(upper, sign * crossed, -sign * crossed)
        )
    return result


def plane_kernel(sign, scale, copies, data_ref, table_ref, out_ref, middle_ref, end_ref):
    table = table_ref[...]
    for x in range(0, NB, 2):
        pair = [data_ref[2 * i : 2 * i + 2].reshape(32, 128) for i in (x, x + 1)]
        for i, rows in enumerate(line_waves(table, pair, sign)):
            middle_ref[(x + i) * 32 : (x + i + 1) * 32, :] = rows
    for y in range(0, NB, 2):
        pair = [middle_ref[pl.ds(i, 32, stride=32), :] for i in (y, y + 1)]
        for i, rows in enumerate(line_waves(table, pair, sign)):
            end_ref[pl.ds(y + i, 32, stride=32), :] = rows
    total = (end_ref[...] * scale).astype(BF16).reshape(64, 16, 128)
    for copy in range(copies):
        out_ref[:, copy] = total


def frequency_kernel(spec_ref, kernel_ref, select_ref, back_ref, out_ref, panel_ref):
    step = pl.program_id(0)

    @pl.when(step == 0)
    def _():
        total = jnp.zeros((512, 512), F32)
        last = jnp.zeros((32, 512), F32)
        for group in range(4):
            panel = spec_ref[:, :, group].reshape(512, 128)
            total += dot(panel, select_ref[group])
            closing = gather_last(panel[0:32].astype(F32), panel[32:64].astype(F32), 32)
            last += dot(closing.astype(BF16), select_ref[group])
        for kz in range(KZ):
            for rhs in range(RHS):
                row = (kz * RHS + rhs) * 16
                rows = total[row : row + 16] if kz < 16 else last[rhs * 16 : rhs * 16 + 16]
                re, im = rows[:, :256].astype(BF16), rows[:, 256:].astype(BF16)
                upper = slice(rhs * 16, rhs * 16 + 16)
                lower = slice(32 + rhs * 16, 48 + rhs * 16)
                panel_ref[kz, upper, 0:256] = re
                panel_ref[kz, lower, 0:256] = im
                panel_ref[kz, upper, 256:512] = -im
                panel_ref[kz, lower, 256:512] = re

    panel = panel_ref[step]
    product = dot_nt(panel[:, 0:152], kernel_ref[0, 0, 0].reshape(1216, 152))
    product += dot_nt(panel[:, 256:408], kernel_ref[1, 0, 0].reshape(1216, 152))
    row = lax.broadcasted_iota(jnp.int32, (64, 1216), 0)
    lane = lax.broadcasted_iota(jnp.int32, (64, 1216), 1)
    own = jnp.where(row % 16 == lane % 16, product, 0.0).astype(BF16)
    weight = jnp.where((step == 0) | (step == 16), 1.0, 2.0).astype(F32)
    local = dot(own, back_ref[...]) * weight
    chunks = []
    for rhs in range(RHS):
        for half in range(2):
            tile = local[:, half * 128 : half * 128 + 128]
            im = pltpu.roll(tile[32 + rhs * 16 : 48 + rhs * 16], 64, 1)
            chunks.append(tile[rhs * 16 : rhs * 16 + 16] + im)

    @pl.when(step < 16)
    def _():
        for group in range(4):
            out_ref[step, group] = chunks[group].astype(BF16)

    @pl.when(step == 16)
    def _():
        for group in range(4):
            for block, extra in enumerate(spread_last(chunks[group], 16)):
                whole = out_ref[block, group].astype(F32) + extra
                out_ref[block, group] = whole.astype(BF16)


def from_z_kernel(scale, data_ref, table_ref, out_ref):
    for group in range(4):
        data = data_ref[:, group].astype(F32)
        first_row = (group // 2 * 76 + group % 2 * HALF) * 4
        for block in range(2):
            rows = data[:, block * 8 : block * 8 + 8, :].reshape(128, 128)
            last = gather_last(rows[0:8], rows[8:16], 8)
            full = jnp.concatenate([rows, last], 0).astype(BF16)
            product = dot_tn(full, table_ref[...])
            total = (product[0:HALF, :256] + product[64 : 64 + HALF, 256:]) * scale
            for part in range(2):
                start = first_row + block * 2 + part
                out_ref[pl.ds(start, HALF, stride=4), :] = total[:, part * 128 : part * 128 + 128]


def vmem(count):
    return [pl.BlockSpec(memory_space=pltpu.VMEM)] * count


def grant(mib):
    return pltpu.CompilerParams(vmem_limit_bytes=mib * 2**20)


def along_z(field, table):
    return pl.pallas_call(
        along_z_kernel,
        out_shape=jax.ShapeDtypeStruct((16, 4, 16, 128), F32),
        in_specs=vmem(2),
        out_specs=pl.BlockSpec(memory_space=pltpu.VMEM),
        scratch_shapes=[pltpu.VMEM((256, 512), BF16)],
        compiler_params=grant(8),
        name="along_z",
    )(field, table)


def planes(data, table, sign, scale, copies, name):
    return pl.pallas_call(
        functools.partial(plane_kernel, sign, scale, copies),
        out_shape=jax.ShapeDtypeStruct((64, copies, 16, 128), BF16),
        in_specs=vmem(2),
        out_specs=pl.BlockSpec(memory_space=pltpu.VMEM),
        scratch_shapes=[pltpu.VMEM((1024, 128), F32), pltpu.VMEM((1024, 128), F32)],
        compiler_params=grant(8),
        name=name,
    )(data, table)


def frequencies(spectrum, kernel, select, back):
    return pl.pallas_call(
        frequency_kernel,
        grid=(KZ,),
        out_shape=jax.ShapeDtypeStruct((16, 4, 16, 128), BF16),
        in_specs=[
            pl.BlockSpec((16, 2, 4, 16, 128), lambda i: (0, 0, 0, 0, 0)),
            pl.BlockSpec((2, 1, 1, 76, 16, 152), lambda i: (0, 0, i, 0, 0, 0)),
            pl.BlockSpec((4, 128, 512), lambda i: (0, 0, 0)),
            pl.BlockSpec((1216, 256), lambda i: (0, 0)),
        ],
        out_specs=pl.BlockSpec((16, 4, 16, 128), lambda i: (0, 0, 0, 0)),
        scratch_shapes=[pltpu.VMEM((KZ, 64, 512), BF16)],
        compiler_params=grant(16),
        name="frequencies",
    )(spectrum, kernel, select, back)


def from_z(data, table, scale):
    return pl.pallas_call(
        functools.partial(from_z_kernel, scale),
        out_shape=jax.ShapeDtypeStruct((608, 128), F32),
        in_specs=vmem(2),
        out_specs=pl.BlockSpec(memory_space=pltpu.VMEM),
        compiler_params=grant(8),
        name="from_z",
    )(data, table)


def exchange(chunks, axes):
    return lax.all_to_all(chunks, axes, 0, 0, tiled=True)


def on_device(multipoles, kernel):
    ahead, behind = (jnp.asarray(t) for t in tables_z())
    table = jnp.asarray(table_line())
    near = ("bx", "by")
    waves = along_z(multipoles.reshape(4, HALF, 512), ahead).reshape(64, 16, 128)
    waves = exchange(waves, near)
    spectrum = planes(waves, table, 1.0, 1.0 / SCALE**3, 2, "to_waves")
    spectrum = exchange(spectrum.reshape(128, 16, 128), ("bx", "by", "col"))
    local = frequencies(
        spectrum.reshape(16, 2, 4, 16, 128),
        kernel.transpose(0, 1, 3, 4, 2, 5),
        jnp.asarray(select_in()),
        jnp.asarray(select_out()),
    )
    local = exchange(local.reshape(64, 16, 128), near)
    back = planes(local, table, -1.0, 1.0 / (1024 * SCALE**2), 1, "from_waves")
    back = exchange(back.reshape(64, 16, 128), near)
    result = from_z(back.reshape(16, 4, 16, 128), behind, 1.0 / (32 * SCALE))
    return result.reshape(multipoles.shape)


def solution(mesh):
    placed = (P(None, "col", "bx", "by"), P(None, "bx", "by", None, "col", None))
    return jax.shard_map(
        on_device, mesh=mesh, in_specs=placed, out_specs=P(None, "col", "bx", "by"), check_vma=False
    )
```

```python
import functools
import math

import jax
import jax.numpy as jnp
import numpy as np
from jax import lax
from jax.experimental import pallas as pl
from jax.experimental.pallas import tpu as pltpu
from jax.sharding import PartitionSpec as P

NB = 32
KZ = 17
RHS = 2
HALF = 38
SPARE = 19
BATCHES = (10, 7)
F32 = jnp.float32
BF16 = jnp.bfloat16


def to_bf16(values):
    return np.asarray(values, np.float32).astype(jnp.bfloat16)


def table_scale():
    level = np.cos(2 * np.pi * np.arange(8) / 32)
    weight = np.array([2.0] + [4.0] * 7)
    scales = np.linspace(1.0, 2.0, 20001)[:-1]
    scaled = scales[:, None] * level[None, :]
    error = to_bf16(scaled).astype(np.float64) / scales[:, None] - level[None, :]
    return float(scales[np.argmin((weight * error**2).sum(1))])


SCALE = table_scale()


def table_back():
    kz = np.arange(KZ)[:, None]
    z = np.arange(NB)[None, :]
    angle = 2 * np.pi * ((kz * z) % NB) / NB
    eye = np.eye(8)
    cos = np.einsum("kz,ab->kabz", np.cos(angle), eye).reshape(KZ * 8, 8 * NB)
    sin = np.einsum("kz,ab->kabz", -np.sin(angle), eye).reshape(KZ * 8, 8 * NB)
    sin[128:] = 0
    return to_bf16(SCALE * np.concatenate([cos, sin], 1))


def iota(shape, axis):
    return lax.broadcasted_iota(jnp.int32, shape, axis)


def cosine(steps):
    return SCALE * jnp.cos((steps % NB).astype(F32) * (2 * math.pi / NB))


def high_part(values):
    return values.astype(BF16).astype(F32)


def line_table():
    row, lane = iota((64, 128), 0), iota((64, 128), 1)
    values = cosine((row % NB) * (lane % NB) - 8 * (row // NB))
    high = high_part(values)
    return jnp.where(lane // NB == 1, values - high, high).astype(BF16)


def ahead_table():
    kz, z = iota((24, 128), 0), iota((24, 128), 1) % NB
    cos = cosine(kz * z)
    sin = cosine(kz * z + 8)
    parts = [(high_part(cos), KZ), (cos - high_part(cos), KZ)]
    parts += [(high_part(sin), 16), (sin - high_part(sin), 16)]
    sides = []
    for side in range(2):
        own = iota((KZ, 8, 128), 1) == iota((KZ, 8, 128), 2) // NB + 4 * side
        blocks = []
        for values, count in parts:
            spread = jnp.broadcast_to(values[:count, None, :], (count, 8, 128))
            blocks.append(jnp.where(own[:count], spread, 0.0).reshape(count * 8, 128))
        sides.append(jnp.concatenate(blocks, 0).astype(BF16))
    return jnp.concatenate(sides, 1)


def select_in(group):
    start = group % 2 * 76 + group // 2 * HALF
    row, lane = iota((128, 512), 0), iota((128, 512), 1)
    real = (row < HALF) & (lane == row + start)
    imag = (row >= 64) & (row < 64 + HALF) & (lane == row + (192 + start))
    return jnp.where(real | imag, 1.0, 0.0).astype(BF16)


def select_out():
    coefficient, lane = iota((1216, 256), 0) // 16, iota((1216, 256), 1)
    target = jnp.where(coefficient < HALF, coefficient, coefficient + 128 - HALF)
    return jnp.where(lane == target, 1.0, 0.0).astype(BF16)


def lane_index(rows):
    return lax.broadcasted_iota(jnp.int32, (rows, 128), 1)


def lanes_between(rows, low, high):
    lane = lane_index(rows) % 64
    return (lane >= low) & (lane < high)


def dot_nt(left, right):
    return lax.dot_general(left, right, (((1,), (1,)), ((), ())), preferred_element_type=F32)


def dot_tn(left, right):
    return lax.dot_general(left, right, (((0,), (0,)), ((), ())), preferred_element_type=F32)


def dot(left, right):
    return jnp.dot(left, right, preferred_element_type=F32)


def spread_last(last, rows, base=0):
    spare = lanes_between(rows, HALF, HALF + SPARE)
    first = jnp.where(spare, pltpu.roll(last, (HALF - base) % 128, 1), 0.0)
    second = jnp.where(spare, pltpu.roll(last, (HALF - SPARE - base) % 128, 1), 0.0)
    return first, second


def gather_last(first, second, rows):
    first = jnp.where(lanes_between(rows, 0, SPARE), pltpu.roll(first, 128 - HALF, 1), 0.0)
    second = jnp.where(
        lanes_between(rows, SPARE, HALF), pltpu.roll(second, 128 - HALF + SPARE, 1), 0.0
    )
    return first + second


def along_z_kernel(field_ref, out_ref, padded_ref):
    table = ahead_table()
    padded_ref[...] = jnp.zeros_like(padded_ref)
    field = field_ref[...].astype(F32)
    for group in range(4):
        half = group % 2 * HALF
        rows = field[half : half + HALF, group // 2, :]
        padded_ref[group * 64 : group * 64 + HALF, :] = rows.astype(BF16)
    lower = lane_index(128) < 64
    spare = lanes_between(8, HALF, HALF + SPARE) & (lane_index(8) < 64)
    for block in range(2):
        product = dot_nt(table, padded_ref[:, block * 256 : block * 256 + 256])
        cos = product[0:136] + product[136:272]
        sin = product[272:400] + product[400:528]
        for group in range(4):
            tile = slice(group // 2 * 128, group // 2 * 128 + 128)
            re, im, last = cos[:128, tile], sin[:, tile], cos[128:, tile]
            if group % 2 == 0:
                im = pltpu.roll(im, 64, 1)
            else:
                re = pltpu.roll(re, 64, 1)
            chunk = jnp.where(lower, re, im).reshape(16, 8, 128)
            first, second = spread_last(last, 8, group % 2 * 64)
            rows = slice(block * 8, block * 8 + 8)
            out_ref[:, group, rows, :] = chunk
            out_ref[0, group, rows, :] = chunk[0] + jnp.where(spare, first, 0.0)
            out_ref[1, group, rows, :] = chunk[1] + jnp.where(spare, second, 0.0)


def line_waves(table, pair, sign):
    both = jnp.concatenate(pair, 1)
    high = both.astype(BF16)
    if both.dtype == BF16:
        stacked = jnp.concatenate([high, high], 0)
    else:
        low = (both - high.astype(F32)).astype(BF16)
        stacked = jnp.concatenate([high, high, low], 0)
    product = dot(table[:, : stacked.shape[0]], stacked)
    upper = lane_index(32) < 64
    result = []
    for lane in (0, 128):
        crossed = pltpu.roll(product[32:, lane : lane + 128], 64, 1)
        result.append(
            product[:32, lane : lane + 128] + jnp.where(upper, sign * crossed, -sign * crossed)
        )
    return result


def plane_kernel(sign, scale, copies, data_ref, out_ref, middle_ref, end_ref):
    table = line_table()
    for x in range(0, NB, 2):
        pair = [data_ref[2 * i : 2 * i + 2].reshape(32, 128) for i in (x, x + 1)]
        for i, rows in enumerate(line_waves(table, pair, sign)):
            middle_ref[(x + i) * 32 : (x + i + 1) * 32, :] = rows
    for y in range(0, NB, 2):
        pair = [middle_ref[pl.ds(i, 32, stride=32), :] for i in (y, y + 1)]
        for i, rows in enumerate(line_waves(table, pair, sign)):
            end_ref[pl.ds(y + i, 32, stride=32), :] = rows
    total = (end_ref[...] * scale).astype(BF16).reshape(64, 16, 128)
    for copy in range(copies):
        out_ref[:, copy] = total


def panels(spec_ref, panel_ref):
    total = jnp.zeros((512, 512), F32)
    last = jnp.zeros((32, 512), F32)
    for group in range(4):
        panel = spec_ref[:, :, group].reshape(512, 128)
        select = select_in(group)
        total += dot(panel, select)
        closing = gather_last(panel[0:32].astype(F32), panel[32:64].astype(F32), 32)
        last += dot(closing.astype(BF16), select)
    for kz in range(KZ):
        for rhs in range(RHS):
            row = (kz * RHS + rhs) * 16
            rows = total[row : row + 16] if kz < 16 else last[rhs * 16 : rhs * 16 + 16]
            re, im = rows[:, :256].astype(BF16), rows[:, 256:].astype(BF16)
            upper = slice(rhs * 16, rhs * 16 + 16)
            lower = slice(32 + rhs * 16, 48 + rhs * 16)
            panel_ref[kz, upper, 0:256] = re
            panel_ref[kz, lower, 0:256] = im
            panel_ref[kz, upper, 256:512] = -im
            panel_ref[kz, lower, 256:512] = re


def frequency_kernel(
    spec_ref, kernel_hbm, out_ref, back_ref, kernel_ref, panel_ref, own_ref, kernel_sem
):
    def load(kz):
        return pltpu.make_async_copy(
            kernel_hbm.at[:, 0, kz], kernel_ref.at[kz], kernel_sem.at[kz]
        )

    for kz in range(KZ):
        load(kz).start()
    panels(spec_ref, panel_ref)
    back_ref[...] = select_out()

    row = lax.broadcasted_iota(jnp.int32, (64, 128), 0)
    lane = lax.broadcasted_iota(jnp.int32, (64, 128), 1)
    same = row % 16 == lane % 16

    def step(kz, carry):
        load(kz).wait()
        panel = panel_ref[kz]
        product = dot_nt(panel[:, 0:152], kernel_ref[kz, 0].reshape(1216, 152))
        product += dot_nt(panel[:, 256:408], kernel_ref[kz, 1].reshape(1216, 152))
        for tile in range(0, 1216, 128):
            wide = min(128, 1216 - tile)
            part = jnp.where(same[:, :wide], product[:, tile : tile + wide], 0.0)
            own_ref[kz, :, tile : tile + wide] = part.astype(BF16)
        return carry

    def finish(first, count):
        local = dot(own_ref[first : first + count].reshape(count * 64, 1216), back_ref[...])
        local = local.reshape(count, 64, 256)
        for kz in range(first, first + count):
            for group in range(4):
                rhs, half = group // 2, group % 2
                tile = local[kz - first, :, half * 128 : half * 128 + 128]
                im = pltpu.roll(tile[32 + rhs * 16 : 48 + rhs * 16], 64, 1)
                chunk = tile[rhs * 16 : rhs * 16 + 16] + im
                if kz in (0, 16):
                    chunk = chunk.astype(BF16)
                else:
                    chunk = (chunk * 2.0).astype(BF16)
                if kz < 16:
                    out_ref[kz, group] = chunk
                else:
                    for block, extra in enumerate(spread_last(chunk.astype(F32), 16)):
                        whole = out_ref[block, group].astype(F32) + extra
                        out_ref[block, group] = whole.astype(BF16)

    first = 0
    for count in BATCHES:
        lax.fori_loop(first, first + count, step, 0)
        finish(first, count)
        first += count


def from_z_kernel(scale, data_ref, table_ref, out_ref):
    for group in range(4):
        data = data_ref[:, group].astype(F32)
        first_row = (group // 2 * 76 + group % 2 * HALF) * 4
        for block in range(2):
            rows = data[:, block * 8 : block * 8 + 8, :].reshape(128, 128)
            last = gather_last(rows[0:8], rows[8:16], 8)
            full = jnp.concatenate([rows, last], 0).astype(BF16)
            product = dot_tn(full, table_ref[...])
            total = (product[0:HALF, :256] + product[64 : 64 + HALF, 256:]) * scale
            for part in range(2):
                start = first_row + block * 2 + part
                out_ref[pl.ds(start, HALF, stride=4), :] = total[:, part * 128 : part * 128 + 128]


def vmem(count):
    return [pl.BlockSpec(memory_space=pltpu.VMEM)] * count


def grant(mib):
    return pltpu.CompilerParams(vmem_limit_bytes=mib * 2**20)


def along_z(field):
    return pl.pallas_call(
        along_z_kernel,
        out_shape=jax.ShapeDtypeStruct((16, 4, 16, 128), F32),
        in_specs=vmem(1),
        out_specs=pl.BlockSpec(memory_space=pltpu.VMEM),
        scratch_shapes=[pltpu.VMEM((256, 512), BF16)],
        compiler_params=grant(8),
        name="along_z",
    )(field)


def planes(data, sign, scale, copies, name):
    return pl.pallas_call(
        functools.partial(plane_kernel, sign, scale, copies),
        out_shape=jax.ShapeDtypeStruct((64, copies, 16, 128), BF16),
        in_specs=vmem(1),
        out_specs=pl.BlockSpec(memory_space=pltpu.VMEM),
        scratch_shapes=[pltpu.VMEM((1024, 128), F32), pltpu.VMEM((1024, 128), F32)],
        compiler_params=grant(8),
        name=name,
    )(data)


def frequencies(spectrum, kernel):
    return pl.pallas_call(
        frequency_kernel,
        out_shape=jax.ShapeDtypeStruct((16, 4, 16, 128), BF16),
        in_specs=vmem(1) + [pl.BlockSpec(memory_space=pltpu.HBM)],
        out_specs=pl.BlockSpec(memory_space=pltpu.VMEM),
        scratch_shapes=[
            pltpu.VMEM((1216, 256), BF16),
            pltpu.VMEM((KZ, 2, 76, 16, 152), BF16),
            pltpu.VMEM((KZ, 64, 512), BF16),
            pltpu.VMEM((KZ, 64, 1216), BF16),
            pltpu.SemaphoreType.DMA((KZ,)),
        ],
        compiler_params=grant(40),
        name="frequencies",
    )(spectrum, kernel)


def from_z(data, table, scale):
    return pl.pallas_call(
        functools.partial(from_z_kernel, scale),
        out_shape=jax.ShapeDtypeStruct((608, 128), F32),
        in_specs=vmem(2),
        out_specs=pl.BlockSpec(memory_space=pltpu.VMEM),
        compiler_params=grant(8),
        name="from_z",
    )(data, table)


def exchange(chunks, axes):
    return lax.all_to_all(chunks, axes, 0, 0, tiled=True)


def on_device(multipoles, kernel):
    near = ("bx", "by")
    waves = along_z(multipoles[:, :, 0, :].transpose(1, 0, 2)).reshape(64, 16, 128)
    waves = exchange(waves, near)
    spectrum = planes(waves, 1.0, 1.0 / SCALE**3, 2, "to_waves")
    spectrum = exchange(spectrum.reshape(128, 16, 128), ("bx", "by", "col"))
    local = frequencies(spectrum.reshape(16, 2, 4, 16, 128), kernel.transpose(0, 1, 3, 4, 2, 5))
    local = exchange(local.reshape(64, 16, 128), near)
    back = planes(local, -1.0, 1.0 / (1024 * SCALE**2), 1, "from_waves")
    back = exchange(back.reshape(64, 16, 128), near)
    behind = jnp.asarray(table_back())
    result = from_z(back.reshape(16, 4, 16, 128), behind, 1.0 / (32 * SCALE))
    return result.reshape(multipoles.shape)


def solution(mesh):
    placed = (P(None, "col", "bx", "by"), P(None, "bx", "by", None, "col", None))
    return jax.shard_map(
        on_device, mesh=mesh, in_specs=placed, out_specs=P(None, "col", "bx", "by"), check_vma=False
    )
```

```python
import functools
import math

import jax
import jax.numpy as jnp
import numpy as np
from jax import lax
from jax.experimental import pallas as pl
from jax.experimental.pallas import tpu as pltpu
from jax.sharding import PartitionSpec as P

NB = 32
KZ = 17
RHS = 2
HALF = 38
SPARE = 19
ROWS = 3
BATCHES = (10, 7)
F32 = jnp.float32
BF16 = jnp.bfloat16


def to_bf16(values):
    return np.asarray(values, np.float32).astype(jnp.bfloat16)


def table_scale():
    level = np.cos(2 * np.pi * np.arange(8) / 32)
    weight = np.array([2.0] + [4.0] * 7)
    scales = np.linspace(1.0, 2.0, 20001)[:-1]
    scaled = scales[:, None] * level[None, :]
    error = to_bf16(scaled).astype(np.float64) / scales[:, None] - level[None, :]
    return float(scales[np.argmin((weight * error**2).sum(1))])


SCALE = table_scale()


def table_back():
    kz = np.arange(KZ)[:, None]
    z = np.arange(NB)[None, :]
    angle = 2 * np.pi * ((kz * z) % NB) / NB
    eye = np.eye(8)
    cos = np.einsum("kz,ab->kabz", np.cos(angle), eye).reshape(KZ * 8, 8 * NB)
    sin = np.einsum("kz,ab->kabz", -np.sin(angle), eye).reshape(KZ * 8, 8 * NB)
    sin[128:] = 0
    return to_bf16(SCALE * np.concatenate([cos, sin], 1))


def iota(shape, axis):
    return lax.broadcasted_iota(jnp.int32, shape, axis)


def cosine(steps):
    return SCALE * jnp.cos((steps % NB).astype(F32) * (2 * math.pi / NB))


def high_part(values):
    return values.astype(BF16).astype(F32)


def line_table():
    row, lane = iota((64, 128), 0), iota((64, 128), 1)
    values = cosine((row % NB) * (lane % NB) - 8 * (row // NB))
    high = high_part(values)
    return jnp.where(lane // NB == 1, values - high, high).astype(BF16)


def ahead_table():
    row, lane = iota((128, 128), 0), iota((128, 128), 1)
    place = lane % 64
    own = (place < ROWS * KZ) & (place // KZ == row // NB)
    values = jnp.where(own, cosine((place % KZ) * (row % NB) + 8 * (lane // 64)), 0.0)
    high = high_part(values)
    return high.astype(BF16), (values - high).astype(BF16)


def select_in():
    line, lane = iota((128 * ROWS, 512), 0), iota((128 * ROWS, 512), 1)
    source = line % 128
    row = source // 2 * ROWS + line // 128
    target = row // 76 * 256 + source % 2 * 76 + row % 76
    return jnp.where((row < 152) & (lane == target), 1.0, 0.0).astype(BF16)


def select_out():
    coefficient, lane = iota((1216, 256), 0) // 16, iota((1216, 256), 1)
    target = jnp.where(coefficient < HALF, coefficient, coefficient + 128 - HALF)
    return jnp.where(lane == target, 1.0, 0.0).astype(BF16)


def lane_index(rows):
    return lax.broadcasted_iota(jnp.int32, (rows, 128), 1)


def lanes_between(rows, low, high):
    lane = lane_index(rows) % 64
    return (lane >= low) & (lane < high)


def dot_nt(left, right):
    return lax.dot_general(left, right, (((1,), (1,)), ((), ())), preferred_element_type=F32)


def dot_tn(left, right):
    return lax.dot_general(left, right, (((0,), (0,)), ((), ())), preferred_element_type=F32)


def dot(left, right):
    return jnp.dot(left, right, preferred_element_type=F32)


def spread_last(last, rows, base=0):
    spare = lanes_between(rows, HALF, HALF + SPARE)
    first = jnp.where(spare, pltpu.roll(last, (HALF - base) % 128, 1), 0.0)
    second = jnp.where(spare, pltpu.roll(last, (HALF - SPARE - base) % 128, 1), 0.0)
    return first, second


def gather_last(first, second, rows):
    first = jnp.where(lanes_between(rows, 0, SPARE), pltpu.roll(first, 128 - HALF, 1), 0.0)
    second = jnp.where(
        lanes_between(rows, SPARE, HALF), pltpu.roll(second, 128 - HALF + SPARE, 1), 0.0
    )
    return first + second


def spread_rows_kernel(field_ref, out_ref, rows_ref, chunk_ref):
    field = field_ref[...].astype(F32)
    rows_ref[:, 152:168, :] = jnp.zeros((4, 16, 128), F32)
    for tile in range(4):
        for rhs in range(RHS):
            part = field[:, rhs, tile * 128 : tile * 128 + 128]
            rows_ref[tile, rhs * 76 : rhs * 76 + 76, :] = part
    chunk_ref[896:1024, :] = jnp.zeros((128, 128), F32)
    slot = lane_index(56) // NB
    for tile in range(4):
        parts = [rows_ref[tile, pl.ds(row, 56, stride=ROWS), :] for row in range(ROWS)]
        for y in range(4):
            total = jnp.zeros((56, 128), F32)
            for row in range(ROWS):
                shift = (row - y) % 4 * NB
                moved = pltpu.roll(parts[row], shift, 1) if shift else parts[row]
                total = jnp.where(slot == row, moved, total)
            chunk_ref[pl.ds(tile * 4 + y, 56, stride=16), :] = total
    out_ref[...] = chunk_ref[...].astype(BF16).reshape(64, 16, 128)


def line_waves(table, pair, sign):
    both = jnp.concatenate(pair, 1)
    high = both.astype(BF16)
    if both.dtype == BF16:
        stacked = jnp.concatenate([high, high], 0)
    else:
        low = (both - high.astype(F32)).astype(BF16)
        stacked = jnp.concatenate([high, high, low], 0)
    product = dot(table[:, : stacked.shape[0]], stacked)
    upper = lane_index(32) < 64
    result = []
    for lane in (0, 128):
        crossed = pltpu.roll(product[32:, lane : lane + 128], 64, 1)
        result.append(
            product[:32, lane : lane + 128] + jnp.where(upper, sign * crossed, -sign * crossed)
        )
    return result


def plane_waves(sign, scale, copies, load, out_ref, middle_ref, end_ref):
    table = line_table()
    for x in range(0, NB, 2):
        pair = [load(i) for i in (x, x + 1)]
        for i, rows in enumerate(line_waves(table, pair, sign)):
            middle_ref[(x + i) * 32 : (x + i + 1) * 32, :] = rows
    for y in range(0, NB, 2):
        pair = [middle_ref[pl.ds(i, 32, stride=32), :] for i in (y, y + 1)]
        for i, rows in enumerate(line_waves(table, pair, sign)):
            end_ref[pl.ds(y + i, 32, stride=32), :] = rows
    total = (end_ref[...] * scale).astype(BF16).reshape(64, 16, 128)
    for copy in range(copies):
        out_ref[:, copy] = total


def to_waves_kernel(data_ref, out_ref, start_ref, middle_ref, end_ref):
    high, low = ahead_table()
    data = data_ref[...].reshape(1024, 128)
    start_ref[...] = dot(data, high) + dot(data, low)

    def load(x):
        return start_ref[x * 32 : x * 32 + 32, :]

    plane_waves(1.0, 1.0 / SCALE**3, 2, load, out_ref, middle_ref, end_ref)


def from_waves_kernel(data_ref, out_ref, middle_ref, end_ref):
    def load(x):
        return data_ref[2 * x : 2 * x + 2].reshape(32, 128)

    plane_waves(-1.0, 1.0 / (1024 * SCALE**2), 1, load, out_ref, middle_ref, end_ref)


def panels(spec_ref, panel_ref, flat_ref, line_ref, whole_ref):
    flat_ref[...] = spec_ref[...].astype(F32).reshape(2048, 128)

    def turn(ky, carry):
        lanes = flat_ref[pl.ds(ky, 128, stride=16), :].T
        for row in range(ROWS):
            for part in range(2):
                start = part * 64 + row * KZ
                place = pl.multiple_of(ky * 48 + part * 24, 8)
                line_ref[row, pl.ds(place, 24), :] = lanes[start : start + 24]
        return carry

    lax.fori_loop(0, 16, turn, 0)
    select = select_in()
    total = dot(line_ref[0].astype(BF16), select[0:128])
    for row in range(1, ROWS):
        total += dot(line_ref[row].astype(BF16), select[row * 128 : row * 128 + 128])
    for tile in range(4):
        whole_ref[tile] = total[:, tile * 128 : tile * 128 + 128]

    def place_panel(kz, carry):
        for rhs in range(RHS):
            upper = slice(rhs * 16, rhs * 16 + 16)
            lower = slice(32 + rhs * 16, 48 + rhs * 16)
            for tile in range(2):
                tiles = whole_ref.at[rhs * 2 + tile]
                re = tiles[pl.ds(kz, 16, stride=48), :].astype(BF16)
                im = tiles[pl.ds(kz + 24, 16, stride=48), :].astype(BF16)
                near = slice(tile * 128, tile * 128 + 128)
                far = slice(256 + tile * 128, 384 + tile * 128)
                panel_ref[kz, upper, near] = re
                panel_ref[kz, lower, near] = im
                panel_ref[kz, upper, far] = -im
                panel_ref[kz, lower, far] = re
        return carry

    lax.fori_loop(0, KZ, place_panel, 0)


def frequency_kernel(
    spec_ref,
    kernel_hbm,
    out_ref,
    back_ref,
    kernel_ref,
    panel_ref,
    own_ref,
    flat_ref,
    line_ref,
    whole_ref,
    kernel_sem,
):
    def load(kz):
        return pltpu.make_async_copy(
            kernel_hbm.at[:, 0, kz], kernel_ref.at[kz], kernel_sem.at[kz]
        )

    for kz in range(KZ):
        load(kz).start()
    panels(spec_ref, panel_ref, flat_ref, line_ref, whole_ref)
    back_ref[...] = select_out()

    row = lax.broadcasted_iota(jnp.int32, (64, 128), 0)
    lane = lax.broadcasted_iota(jnp.int32, (64, 128), 1)
    same = row % 16 == lane % 16

    def step(kz, carry):
        load(kz).wait()
        panel = panel_ref[kz]
        product = dot_nt(panel[:, 0:152], kernel_ref[kz, 0].reshape(1216, 152))
        product += dot_nt(panel[:, 256:408], kernel_ref[kz, 1].reshape(1216, 152))
        for tile in range(0, 1216, 128):
            wide = min(128, 1216 - tile)
            part = jnp.where(same[:, :wide], product[:, tile : tile + wide], 0.0)
            own_ref[kz, :, tile : tile + wide] = part.astype(BF16)
        return carry

    def finish(first, count):
        local = dot(own_ref[first : first + count].reshape(count * 64, 1216), back_ref[...])
        local = local.reshape(count, 64, 256)
        for kz in range(first, first + count):
            for group in range(4):
                rhs, half = group // 2, group % 2
                tile = local[kz - first, :, half * 128 : half * 128 + 128]
                im = pltpu.roll(tile[32 + rhs * 16 : 48 + rhs * 16], 64, 1)
                chunk = tile[rhs * 16 : rhs * 16 + 16] + im
                if kz in (0, 16):
                    chunk = chunk.astype(BF16)
                else:
                    chunk = (chunk * 2.0).astype(BF16)
                if kz < 16:
                    out_ref[kz, group] = chunk
                else:
                    for block, extra in enumerate(spread_last(chunk.astype(F32), 16)):
                        whole = out_ref[block, group].astype(F32) + extra
                        out_ref[block, group] = whole.astype(BF16)

    first = 0
    for count in BATCHES:
        lax.fori_loop(first, first + count, step, 0)
        finish(first, count)
        first += count


def from_z_kernel(scale, data_ref, table_ref, out_ref):
    for group in range(4):
        data = data_ref[:, group].astype(F32)
        first_row = (group // 2 * 76 + group % 2 * HALF) * 4
        for block in range(2):
            rows = data[:, block * 8 : block * 8 + 8, :].reshape(128, 128)
            last = gather_last(rows[0:8], rows[8:16], 8)
            full = jnp.concatenate([rows, last], 0).astype(BF16)
            product = dot_tn(full, table_ref[...])
            total = (product[0:HALF, :256] + product[64 : 64 + HALF, 256:]) * scale
            for part in range(2):
                start = first_row + block * 2 + part
                out_ref[pl.ds(start, HALF, stride=4), :] = total[:, part * 128 : part * 128 + 128]


def vmem(count):
    return [pl.BlockSpec(memory_space=pltpu.VMEM)] * count


def grant(mib):
    return pltpu.CompilerParams(vmem_limit_bytes=mib * 2**20)


def local_call(kernel, name, result, scratch, *operands):
    return pl.pallas_call(
        kernel,
        out_shape=result,
        in_specs=vmem(len(operands)),
        out_specs=pl.BlockSpec(memory_space=pltpu.VMEM),
        scratch_shapes=[pltpu.VMEM(shape, F32) for shape in scratch],
        compiler_params=grant(8),
        name=name,
    )(*operands)


def chunks_of(*shape):
    return jax.ShapeDtypeStruct(shape, BF16)


def frequencies(spectrum, kernel):
    return pl.pallas_call(
        frequency_kernel,
        out_shape=jax.ShapeDtypeStruct((16, 4, 16, 128), BF16),
        in_specs=vmem(1) + [pl.BlockSpec(memory_space=pltpu.HBM)],
        out_specs=pl.BlockSpec(memory_space=pltpu.VMEM),
        scratch_shapes=[
            pltpu.VMEM((1216, 256), BF16),
            pltpu.VMEM((KZ, 2, 76, 16, 152), BF16),
            pltpu.VMEM((KZ, 64, 512), BF16),
            pltpu.VMEM((KZ, 64, 1216), BF16),
            pltpu.VMEM((2048, 128), F32),
            pltpu.VMEM((ROWS, 768, 128), F32),
            pltpu.VMEM((4, 768, 128), F32),
            pltpu.SemaphoreType.DMA((KZ,)),
        ],
        compiler_params=grant(40),
        name="frequencies",
    )(spectrum, kernel)


def from_z(data, table, scale):
    return pl.pallas_call(
        functools.partial(from_z_kernel, scale),
        out_shape=jax.ShapeDtypeStruct((608, 128), F32),
        in_specs=vmem(2),
        out_specs=pl.BlockSpec(memory_space=pltpu.VMEM),
        compiler_params=grant(8),
        name="from_z",
    )(data, table)


def exchange(chunks, axes):
    return lax.all_to_all(chunks, axes, 0, 0, tiled=True)


def on_device(multipoles, kernel):
    near = ("bx", "by")
    plane = (1024, 128)
    field = multipoles[:, :, 0, :].transpose(1, 0, 2)
    rows = local_call(
        spread_rows_kernel, "spread_rows", chunks_of(64, 16, 128), [(4, 168, 128), plane], field
    )
    rows = exchange(rows, near)
    spectrum = local_call(
        to_waves_kernel, "to_waves", chunks_of(64, 2, 16, 128), [plane, plane, plane], rows
    )
    spectrum = exchange(spectrum.reshape(128, 16, 128), ("bx", "by", "col"))
    local = frequencies(spectrum, kernel.transpose(0, 1, 3, 4, 2, 5))
    local = exchange(local.reshape(64, 16, 128), near)
    back = local_call(
        from_waves_kernel, "from_waves", chunks_of(64, 1, 16, 128), [plane, plane], local
    )
    back = exchange(back.reshape(64, 16, 128), near)
    behind = jnp.asarray(table_back())
    result = from_z(back.reshape(16, 4, 16, 128), behind, 1.0 / (32 * SCALE))
    return result.reshape(multipoles.shape)


def solution(mesh):
    placed = (P(None, "col", "bx", "by"), P(None, "bx", "by", None, "col", None))
    return jax.shard_map(
        on_device, mesh=mesh, in_specs=placed, out_specs=P(None, "col", "bx", "by"), check_vma=False
    )
```

```python
import functools
import math

import jax
import jax.numpy as jnp
import numpy as np
from jax import lax
from jax.experimental import pallas as pl
from jax.experimental.pallas import tpu as pltpu
from jax.sharding import PartitionSpec as P

NB = 32
KZ = 17
RHS = 2
HALF = 38
SPARE = 19
ROWS = 3
F32 = jnp.float32
BF16 = jnp.bfloat16


def to_bf16(values):
    return np.asarray(values, np.float32).astype(jnp.bfloat16)


def table_scale():
    level = np.cos(2 * np.pi * np.arange(8) / 32)
    weight = np.array([2.0] + [4.0] * 7)
    scales = np.linspace(1.0, 2.0, 20001)[:-1]
    scaled = scales[:, None] * level[None, :]
    error = to_bf16(scaled).astype(np.float64) / scales[:, None] - level[None, :]
    return float(scales[np.argmin((weight * error**2).sum(1))])


SCALE = table_scale()


def table_back():
    kz = np.arange(KZ)[:, None]
    z = np.arange(NB)[None, :]
    angle = 2 * np.pi * ((kz * z) % NB) / NB
    eye = np.eye(8)
    cos = np.einsum("kz,ab->kabz", np.cos(angle), eye).reshape(KZ * 8, 8 * NB)
    sin = np.einsum("kz,ab->kabz", -np.sin(angle), eye).reshape(KZ * 8, 8 * NB)
    sin[128:] = 0
    return to_bf16(SCALE * np.concatenate([cos, sin], 1))


def iota(shape, axis):
    return lax.broadcasted_iota(jnp.int32, shape, axis)


def cosine(steps):
    return SCALE * jnp.cos((steps % NB).astype(F32) * (2 * math.pi / NB))


def high_part(values):
    return values.astype(BF16).astype(F32)


def line_table():
    row, lane = iota((64, 128), 0), iota((64, 128), 1)
    values = cosine((row % NB) * (lane % NB) - 8 * (row // NB))
    high = high_part(values)
    return jnp.where(lane // NB == 1, values - high, high).astype(BF16)


def ahead_table():
    row, lane = iota((128, 128), 0), iota((128, 128), 1)
    place = lane % 64
    own = (place < ROWS * KZ) & (place // KZ == row // NB)
    values = jnp.where(own, cosine((place % KZ) * (row % NB) + 8 * (lane // 64)), 0.0)
    high = high_part(values)
    return high.astype(BF16), (values - high).astype(BF16)


def select_in():
    line, lane = iota((128 * ROWS, 512), 0), iota((128 * ROWS, 512), 1)
    source = line % 128
    row = source // 2 * ROWS + line // 128
    target = row // 76 * 256 + source % 2 * 76 + row % 76
    return jnp.where((row < 152) & (lane == target), 1.0, 0.0).astype(BF16)


def pick_table():
    line, lane = iota((144, 128), 0), iota((144, 128), 1)
    block, kz = line // 24, line % 24
    return jnp.where((kz < KZ) & (lane == block % 2 * 64 + block // 2 * KZ + kz), 1.0, 0.0).astype(
        BF16
    )


def select_out():
    coefficient, lane = iota((1216, 256), 0) // 16, iota((1216, 256), 1)
    target = jnp.where(coefficient < HALF, coefficient, coefficient + 128 - HALF)
    return jnp.where(lane == target, 1.0, 0.0).astype(BF16)


def lane_index(rows):
    return lax.broadcasted_iota(jnp.int32, (rows, 128), 1)


def lanes_between(rows, low, high):
    lane = lane_index(rows) % 64
    return (lane >= low) & (lane < high)


def dot_nt(left, right):
    return lax.dot_general(left, right, (((1,), (1,)), ((), ())), preferred_element_type=F32)


def dot_tn(left, right):
    return lax.dot_general(left, right, (((0,), (0,)), ((), ())), preferred_element_type=F32)


def dot(left, right):
    return jnp.dot(left, right, preferred_element_type=F32)


def spread_last(last, rows, base=0):
    spare = lanes_between(rows, HALF, HALF + SPARE)
    first = jnp.where(spare, pltpu.roll(last, (HALF - base) % 128, 1), 0.0)
    second = jnp.where(spare, pltpu.roll(last, (HALF - SPARE - base) % 128, 1), 0.0)
    return first, second


def gather_last(first, second, rows):
    first = jnp.where(lanes_between(rows, 0, SPARE), pltpu.roll(first, 128 - HALF, 1), 0.0)
    second = jnp.where(
        lanes_between(rows, SPARE, HALF), pltpu.roll(second, 128 - HALF + SPARE, 1), 0.0
    )
    return first + second


def spread_rows_kernel(field_ref, out_ref, rows_ref, chunk_ref):
    field = field_ref[...].astype(F32)
    rows_ref[:, 152:168, :] = jnp.zeros((4, 16, 128), F32)
    for tile in range(4):
        for rhs in range(RHS):
            part = field[:, rhs, tile * 128 : tile * 128 + 128]
            rows_ref[tile, rhs * 76 : rhs * 76 + 76, :] = part
    chunk_ref[896:1024, :] = jnp.zeros((128, 128), F32)
    slot = lane_index(56) // NB
    for tile in range(4):
        parts = [rows_ref[tile, pl.ds(row, 56, stride=ROWS), :] for row in range(ROWS)]
        for y in range(4):
            total = jnp.zeros((56, 128), F32)
            for row in range(ROWS):
                shift = (row - y) % 4 * NB
                moved = pltpu.roll(parts[row], shift, 1) if shift else parts[row]
                total = jnp.where(slot == row, moved, total)
            chunk_ref[pl.ds(tile * 4 + y, 56, stride=16), :] = total
    out_ref[...] = chunk_ref[...].astype(BF16).reshape(64, 16, 128)


def line_waves(table, pair, sign):
    both = jnp.concatenate(pair, 1)
    high = both.astype(BF16)
    if both.dtype == BF16:
        stacked = jnp.concatenate([high, high], 0)
    else:
        low = (both - high.astype(F32)).astype(BF16)
        stacked = jnp.concatenate([high, high, low], 0)
    product = dot(table[:, : stacked.shape[0]], stacked)
    upper = lane_index(32) < 64
    result = []
    for lane in (0, 128):
        crossed = pltpu.roll(product[32:, lane : lane + 128], 64, 1)
        result.append(
            product[:32, lane : lane + 128] + jnp.where(upper, sign * crossed, -sign * crossed)
        )
    return result


def plane_waves(sign, scale, copies, load, out_ref, middle_ref, end_ref):
    table = line_table()
    for x in range(0, NB, 2):
        pair = [load(i) for i in (x, x + 1)]
        for i, rows in enumerate(line_waves(table, pair, sign)):
            middle_ref[(x + i) * 32 : (x + i + 1) * 32, :] = rows
    for y in range(0, NB, 2):
        pair = [middle_ref[pl.ds(i, 32, stride=32), :] for i in (y, y + 1)]
        for i, rows in enumerate(line_waves(table, pair, sign)):
            end_ref[pl.ds(y + i, 32, stride=32), :] = rows
    total = (end_ref[...] * scale).astype(BF16).reshape(64, 16, 128)
    for copy in range(copies):
        out_ref[:, copy] = total


def to_waves_kernel(data_ref, out_ref, start_ref, middle_ref, end_ref):
    high, low = ahead_table()
    data = data_ref[...].reshape(1024, 128)
    start_ref[...] = dot(data, high) + dot(data, low)

    def load(x):
        return start_ref[x * 32 : x * 32 + 32, :]

    plane_waves(1.0, 1.0 / SCALE**3, 2, load, out_ref, middle_ref, end_ref)


def from_waves_kernel(data_ref, out_ref, middle_ref, end_ref):
    def load(x):
        return data_ref[2 * x : 2 * x + 2].reshape(32, 128)

    plane_waves(-1.0, 1.0 / (1024 * SCALE**2), 1, load, out_ref, middle_ref, end_ref)


def panels(spec_ref, panel_ref, flat_ref, line_ref):
    flat_ref[...] = spec_ref[...].astype(F32).reshape(2048, 128)
    pick = pick_table()
    for ky in range(0, 16, 2):
        both = [flat_ref[pl.ds(i, 128, stride=16), :] for i in (ky, ky + 1)]
        turned = dot_nt(pick, jnp.concatenate(both, 0).astype(BF16))
        for i in range(2):
            for row in range(ROWS):
                for part in range(2):
                    block = turned[(row * 2 + part) * 24 : (row * 2 + part) * 24 + 24]
                    place = pl.ds(part * 16 + ky + i, 24, stride=32)
                    line_ref[row, place, :] = block[:, i * 128 : i * 128 + 128]
    lines = [line_ref[row, 0 : KZ * 32, :].astype(BF16) for row in range(ROWS)]
    total = dot(jnp.concatenate(lines, 1), select_in()).astype(BF16)
    for kz in range(KZ):
        re = total[kz * 32 : kz * 32 + 16]
        im = total[kz * 32 + 16 : kz * 32 + 32]
        for rhs in range(RHS):
            lanes = slice(rhs * 256, rhs * 256 + 256)
            upper = slice(rhs * 16, rhs * 16 + 16)
            lower = slice(32 + rhs * 16, 48 + rhs * 16)
            panel_ref[kz, upper, 0:256] = re[:, lanes]
            panel_ref[kz, lower, 0:256] = im[:, lanes]
            panel_ref[kz, upper, 256:512] = -im[:, lanes]
            panel_ref[kz, lower, 256:512] = re[:, lanes]


def frequency_kernel(
    spec_ref,
    kernel_hbm,
    out_ref,
    back_ref,
    kernel_ref,
    panel_ref,
    own_ref,
    flat_ref,
    line_ref,
    kernel_sem,
):
    def load(kz):
        return pltpu.make_async_copy(
            kernel_hbm.at[:, 0, kz], kernel_ref.at[kz], kernel_sem.at[kz]
        )

    for kz in range(KZ):
        load(kz).start()
    panels(spec_ref, panel_ref, flat_ref, line_ref)
    back_ref[...] = select_out()

    row = lax.broadcasted_iota(jnp.int32, (64, 128), 0)
    lane = lax.broadcasted_iota(jnp.int32, (64, 128), 1)
    same = row % 16 == lane % 16

    def step(kz):
        panel = panel_ref[kz]
        product = dot_nt(panel[:, 0:152], kernel_ref[kz, 0].reshape(1216, 152))
        product += dot_nt(panel[:, 256:408], kernel_ref[kz, 1].reshape(1216, 152))
        for tile in range(0, 1216, 128):
            wide = min(128, 1216 - tile)
            part = jnp.where(same[:, :wide], product[:, tile : tile + wide], 0.0)
            own_ref[kz, :, tile : tile + wide] = part.astype(BF16)

    def pair(half, carry):
        for kz in (2 * half, 2 * half + 1):
            load(kz).wait()
        for kz in (2 * half, 2 * half + 1):
            step(kz)
        return carry

    lax.fori_loop(0, KZ // 2, pair, 0)
    load(KZ - 1).wait()
    step(KZ - 1)

    local = dot(own_ref[...].reshape(KZ * 64, 1216), back_ref[...]).reshape(KZ, 64, 256)
    for kz in range(KZ):
        for group in range(4):
            rhs, half = group // 2, group % 2
            tile = local[kz, :, half * 128 : half * 128 + 128]
            im = pltpu.roll(tile[32 + rhs * 16 : 48 + rhs * 16], 64, 1)
            chunk = tile[rhs * 16 : rhs * 16 + 16] + im
            if kz not in (0, 16):
                chunk = chunk * 2.0
            if kz < 16:
                out_ref[kz, group] = chunk.astype(BF16)
            else:
                for block, extra in enumerate(spread_last(chunk, 16)):
                    whole = out_ref[block, group].astype(F32) + extra
                    out_ref[block, group] = whole.astype(BF16)


def from_z_kernel(scale, data_ref, table_ref, out_ref):
    for group in range(4):
        data = data_ref[:, group].astype(F32)
        first_row = (group // 2 * 76 + group % 2 * HALF) * 4
        for block in range(2):
            rows = data[:, block * 8 : block * 8 + 8, :].reshape(128, 128)
            last = gather_last(rows[0:8], rows[8:16], 8)
            full = jnp.concatenate([rows, last], 0).astype(BF16)
            product = dot_tn(full, table_ref[...])
            total = (product[0:HALF, :256] + product[64 : 64 + HALF, 256:]) * scale
            for part in range(2):
                start = first_row + block * 2 + part
                out_ref[pl.ds(start, HALF, stride=4), :] = total[:, part * 128 : part * 128 + 128]


def vmem(count):
    return [pl.BlockSpec(memory_space=pltpu.VMEM)] * count


def grant(mib):
    return pltpu.CompilerParams(vmem_limit_bytes=mib * 2**20)


def local_call(kernel, name, result, scratch, *operands):
    return pl.pallas_call(
        kernel,
        out_shape=result,
        in_specs=vmem(len(operands)),
        out_specs=pl.BlockSpec(memory_space=pltpu.VMEM),
        scratch_shapes=[pltpu.VMEM(shape, F32) for shape in scratch],
        compiler_params=grant(8),
        name=name,
    )(*operands)


def chunks_of(*shape):
    return jax.ShapeDtypeStruct(shape, BF16)


def frequencies(spectrum, kernel):
    return pl.pallas_call(
        frequency_kernel,
        out_shape=jax.ShapeDtypeStruct((16, 4, 16, 128), BF16),
        in_specs=vmem(1) + [pl.BlockSpec(memory_space=pltpu.HBM)],
        out_specs=pl.BlockSpec(memory_space=pltpu.VMEM),
        scratch_shapes=[
            pltpu.VMEM((1216, 256), BF16),
            pltpu.VMEM((KZ, 2, 76, 16, 152), BF16),
            pltpu.VMEM((KZ, 64, 512), BF16),
            pltpu.VMEM((KZ, 64, 1216), BF16),
            pltpu.VMEM((2048, 128), F32),
            pltpu.VMEM((ROWS, 768, 128), F32),
            pltpu.SemaphoreType.DMA((KZ,)),
        ],
        compiler_params=grant(40),
        name="frequencies",
    )(spectrum, kernel)


def from_z(data, table, scale):
    return pl.pallas_call(
        functools.partial(from_z_kernel, scale),
        out_shape=jax.ShapeDtypeStruct((608, 128), F32),
        in_specs=vmem(2),
        out_specs=pl.BlockSpec(memory_space=pltpu.VMEM),
        compiler_params=grant(8),
        name="from_z",
    )(data, table)


def exchange(chunks, axes):
    return lax.all_to_all(chunks, axes, 0, 0, tiled=True)


def on_device(multipoles, kernel):
    near = ("bx", "by")
    plane = (1024, 128)
    field = multipoles[:, :, 0, :].transpose(1, 0, 2)
    rows = local_call(
        spread_rows_kernel, "spread_rows", chunks_of(64, 16, 128), [(4, 168, 128), plane], field
    )
    rows = exchange(rows, near)
    spectrum = local_call(
        to_waves_kernel, "to_waves", chunks_of(64, 2, 16, 128), [plane, plane, plane], rows
    )
    spectrum = exchange(spectrum.reshape(128, 16, 128), ("bx", "by", "col"))
    local = frequencies(spectrum, kernel.transpose(0, 1, 3, 4, 2, 5))
    local = exchange(local.reshape(64, 16, 128), near)
    back = local_call(
        from_waves_kernel, "from_waves", chunks_of(64, 1, 16, 128), [plane, plane], local
    )
    back = exchange(back.reshape(64, 16, 128), near)
    behind = jnp.asarray(table_back())
    result = from_z(back.reshape(16, 4, 16, 128), behind, 1.0 / (32 * SCALE))
    return result.reshape(multipoles.shape)


def solution(mesh):
    placed = (P(None, "col", "bx", "by"), P(None, "bx", "by", None, "col", None))
    return jax.shard_map(
        on_device, mesh=mesh, in_specs=placed, out_specs=P(None, "col", "bx", "by"), check_vma=False
    )
```

```python
import functools
import math

import jax
import jax.numpy as jnp
import numpy as np
from jax import lax
from jax.experimental import pallas as pl
from jax.experimental.pallas import tpu as pltpu
from jax.sharding import PartitionSpec as P

NB = 32
KZ = 17
RHS = 2
HALF = 38
SPARE = 19
ROWS = 3
F32 = jnp.float32
BF16 = jnp.bfloat16


def to_bf16(values):
    return np.asarray(values, np.float32).astype(jnp.bfloat16)


def table_scale():
    level = np.cos(2 * np.pi * np.arange(8) / 32)
    weight = np.array([2.0] + [4.0] * 7)
    scales = np.linspace(1.0, 2.0, 20001)[:-1]
    scaled = scales[:, None] * level[None, :]
    error = to_bf16(scaled).astype(np.float64) / scales[:, None] - level[None, :]
    return float(scales[np.argmin((weight * error**2).sum(1))])


SCALE = table_scale()


def table_back():
    kz = np.arange(KZ)[:, None]
    z = np.arange(NB)[None, :]
    angle = 2 * np.pi * ((kz * z) % NB) / NB
    eye = np.eye(8)
    cos = np.einsum("kz,ab->kabz", np.cos(angle), eye).reshape(KZ * 8, 8 * NB)
    sin = np.einsum("kz,ab->kabz", -np.sin(angle), eye).reshape(KZ * 8, 8 * NB)
    sin[128:] = 0
    return to_bf16(SCALE * np.concatenate([cos, sin], 1))


def iota(shape, axis):
    return lax.broadcasted_iota(jnp.int32, shape, axis)


def cosine(steps):
    return SCALE * jnp.cos((steps % NB).astype(F32) * (2 * math.pi / NB))


def high_part(values):
    return values.astype(BF16).astype(F32)


def line_table():
    row, lane = iota((64, 128), 0), iota((64, 128), 1)
    values = cosine((row % NB) * (lane % NB) - 8 * (row // NB))
    high = high_part(values)
    return jnp.where(lane // NB == 1, values - high, high).astype(BF16)


def ahead_table():
    row, lane = iota((128, 128), 0), iota((128, 128), 1)
    place = lane % 64
    own = (place < ROWS * KZ) & (place // KZ == row // NB)
    values = jnp.where(own, cosine((place % KZ) * (row % NB) + 8 * (lane // 64)), 0.0)
    high = high_part(values)
    return high.astype(BF16), (values - high).astype(BF16)


def select_in():
    line, lane = iota((128 * ROWS, 512), 0), iota((128 * ROWS, 512), 1)
    source = line % 128
    row = source // 2 * ROWS + line // 128
    target = row // 76 * 256 + source % 2 * 76 + row % 76
    return jnp.where((row < 152) & (lane == target), 1.0, 0.0).astype(BF16)


def pick_table():
    line, lane = iota((144, 128), 0), iota((144, 128), 1)
    block, kz = line // 24, line % 24
    return jnp.where((kz < KZ) & (lane == block % 2 * 64 + block // 2 * KZ + kz), 1.0, 0.0).astype(
        BF16
    )


def select_out():
    coefficient, lane = iota((1216, 256), 0) // 16, iota((1216, 256), 1)
    target = jnp.where(coefficient < HALF, coefficient, coefficient + 128 - HALF)
    return jnp.where(lane == target, 1.0, 0.0).astype(BF16)


def lane_index(rows):
    return lax.broadcasted_iota(jnp.int32, (rows, 128), 1)


def lanes_between(rows, low, high):
    lane = lane_index(rows) % 64
    return (lane >= low) & (lane < high)


def dot_nt(left, right):
    return lax.dot_general(left, right, (((1,), (1,)), ((), ())), preferred_element_type=F32)


def dot_tn(left, right):
    return lax.dot_general(left, right, (((0,), (0,)), ((), ())), preferred_element_type=F32)


def dot(left, right):
    return jnp.dot(left, right, preferred_element_type=F32)


def spread_last(last, rows, base=0):
    spare = lanes_between(rows, HALF, HALF + SPARE)
    first = jnp.where(spare, pltpu.roll(last, (HALF - base) % 128, 1), 0.0)
    second = jnp.where(spare, pltpu.roll(last, (HALF - SPARE - base) % 128, 1), 0.0)
    return first, second


def gather_last(first, second, rows):
    first = jnp.where(lanes_between(rows, 0, SPARE), pltpu.roll(first, 128 - HALF, 1), 0.0)
    second = jnp.where(
        lanes_between(rows, SPARE, HALF), pltpu.roll(second, 128 - HALF + SPARE, 1), 0.0
    )
    return first + second


def spread_rows_kernel(field_ref, out_ref, rows_ref, chunk_ref):
    field = field_ref[...].astype(F32)
    rows_ref[:, 152:168, :] = jnp.zeros((4, 16, 128), F32)
    for tile in range(4):
        for rhs in range(RHS):
            part = field[:, rhs, tile * 128 : tile * 128 + 128]
            rows_ref[tile, rhs * 76 : rhs * 76 + 76, :] = part
    chunk_ref[896:1024, :] = jnp.zeros((128, 128), F32)
    slot = lane_index(56) // NB
    for tile in range(4):
        parts = [rows_ref[tile, pl.ds(row, 56, stride=ROWS), :] for row in range(ROWS)]
        for y in range(4):
            total = jnp.zeros((56, 128), F32)
            for row in range(ROWS):
                shift = (row - y) % 4 * NB
                moved = pltpu.roll(parts[row], shift, 1) if shift else parts[row]
                total = jnp.where(slot == row, moved, total)
            chunk_ref[pl.ds(tile * 4 + y, 56, stride=16), :] = total
    out_ref[...] = chunk_ref[...].astype(BF16).reshape(64, 16, 128)


def line_waves(table, pair, sign):
    both = jnp.concatenate(pair, 1)
    high = both.astype(BF16)
    if both.dtype == BF16:
        stacked = jnp.concatenate([high, high], 0)
    else:
        low = (both - high.astype(F32)).astype(BF16)
        stacked = jnp.concatenate([high, high, low], 0)
    product = dot(table[:, : stacked.shape[0]], stacked)
    upper = lane_index(32) < 64
    result = []
    for lane in (0, 128):
        crossed = pltpu.roll(product[32:, lane : lane + 128], 64, 1)
        result.append(
            product[:32, lane : lane + 128] + jnp.where(upper, sign * crossed, -sign * crossed)
        )
    return result


def turned(values, steps, sign, lower):
    if steps == 0:
        return values
    cos = math.cos(2 * math.pi * steps / NB)
    sin = sign * math.sin(2 * math.pi * steps / NB)
    crossed = pltpu.roll(values, 64, 1) * jnp.where(lower, sin, -sin).astype(F32)
    return crossed if steps == 8 else values * cos + crossed


def short_waves(blocks, sign, lower):
    count = len(blocks)
    if count == 1:
        return blocks
    even = short_waves(blocks[0::2], sign, lower)
    odd = short_waves(blocks[1::2], sign, lower)
    odd = [turned(odd[k], k * (NB // count), sign, lower) for k in range(count // 2)]
    return [e + o for e, o in zip(even, odd)] + [e - o for e, o in zip(even, odd)]


def plane_waves(sign, scale, copies, load, out_ref, middle_ref, end_ref):
    table = line_table()
    for x in range(0, NB, 2):
        pair = [load(i) for i in (x, x + 1)]
        for i, rows in enumerate(line_waves(table, pair, sign)):
            middle_ref[(x + i) * 32 : (x + i + 1) * 32, :] = rows
    lower = lane_index(8) < 64

    def column(place, carry):
        start = pl.multiple_of(place * 8, 8)
        blocks = [middle_ref[pl.ds(start + x * 32, 8), :] for x in range(NB)]
        for x, block in enumerate(short_waves(blocks, sign, lower)):
            end_ref[pl.ds(start + x * 32, 8), :] = block
        return carry

    lax.fori_loop(0, 4, column, 0)
    total = (end_ref[...] * scale).astype(BF16).reshape(64, 16, 128)
    for copy in range(copies):
        out_ref[:, copy] = total


def to_waves_kernel(data_ref, out_ref, start_ref, middle_ref, end_ref):
    high, low = ahead_table()
    data = data_ref[...].reshape(1024, 128)
    start_ref[...] = dot(jnp.concatenate([data, data], 1), jnp.concatenate([high, low], 0))

    def load(x):
        return start_ref[x * 32 : x * 32 + 32, :]

    plane_waves(1.0, 1.0 / SCALE**2, 2, load, out_ref, middle_ref, end_ref)


def from_waves_kernel(data_ref, out_ref, middle_ref, end_ref):
    def load(x):
        return data_ref[2 * x : 2 * x + 2].reshape(32, 128)

    plane_waves(-1.0, 1.0 / (1024 * SCALE), 1, load, out_ref, middle_ref, end_ref)


def panels(spec_ref, panel_ref, flat_ref, line_ref):
    flat_ref[...] = spec_ref[...].astype(F32).reshape(2048, 128)
    pick = pick_table()
    for ky in range(0, 16, 2):
        both = [flat_ref[pl.ds(i, 128, stride=16), :] for i in (ky, ky + 1)]
        turned = dot_nt(pick, jnp.concatenate(both, 0).astype(BF16))
        for i in range(2):
            for row in range(ROWS):
                for part in range(2):
                    block = turned[(row * 2 + part) * 24 : (row * 2 + part) * 24 + 24]
                    place = pl.ds(part * 16 + ky + i, 24, stride=32)
                    line_ref[row, place, :] = block[:, i * 128 : i * 128 + 128]
    lines = [line_ref[row, 0 : KZ * 32, :].astype(BF16) for row in range(ROWS)]
    total = dot(jnp.concatenate(lines, 1), select_in()).astype(BF16)
    for kz in range(KZ):
        re = total[kz * 32 : kz * 32 + 16]
        im = total[kz * 32 + 16 : kz * 32 + 32]
        for rhs in range(RHS):
            lanes = slice(rhs * 256, rhs * 256 + 256)
            upper = slice(rhs * 16, rhs * 16 + 16)
            lower = slice(32 + rhs * 16, 48 + rhs * 16)
            panel_ref[kz, upper, 0:256] = re[:, lanes]
            panel_ref[kz, lower, 0:256] = im[:, lanes]
            panel_ref[kz, upper, 256:512] = -im[:, lanes]
            panel_ref[kz, lower, 256:512] = re[:, lanes]


def frequency_kernel(
    spec_ref,
    kernel_hbm,
    out_ref,
    back_ref,
    kernel_ref,
    panel_ref,
    own_ref,
    flat_ref,
    line_ref,
    kernel_sem,
):
    def load(kz):
        return pltpu.make_async_copy(
            kernel_hbm.at[:, 0, kz], kernel_ref.at[kz], kernel_sem.at[kz]
        )

    for kz in range(KZ):
        load(kz).start()
    panels(spec_ref, panel_ref, flat_ref, line_ref)
    back_ref[...] = select_out()

    row = lax.broadcasted_iota(jnp.int32, (64, 128), 0)
    lane = lax.broadcasted_iota(jnp.int32, (64, 128), 1)
    same = row % 16 == lane % 16

    def step(kz):
        panel = panel_ref[kz]
        product = dot_nt(panel[:, 0:152], kernel_ref[kz, 0].reshape(1216, 152))
        product += dot_nt(panel[:, 256:408], kernel_ref[kz, 1].reshape(1216, 152))
        for tile in range(0, 1216, 128):
            wide = min(128, 1216 - tile)
            part = jnp.where(same[:, :wide], product[:, tile : tile + wide], 0.0)
            own_ref[kz, :, tile : tile + wide] = part.astype(BF16)

    def pair(half, carry):
        for kz in (2 * half, 2 * half + 1):
            load(kz).wait()
        for kz in (2 * half, 2 * half + 1):
            step(kz)
        return carry

    lax.fori_loop(0, KZ // 2, pair, 0)
    load(KZ - 1).wait()
    step(KZ - 1)

    local = dot(own_ref[...].reshape(KZ * 64, 1216), back_ref[...]).reshape(KZ, 64, 256)
    for kz in range(KZ):
        for group in range(4):
            rhs, half = group // 2, group % 2
            tile = local[kz, :, half * 128 : half * 128 + 128]
            im = pltpu.roll(tile[32 + rhs * 16 : 48 + rhs * 16], 64, 1)
            chunk = tile[rhs * 16 : rhs * 16 + 16] + im
            if kz not in (0, 16):
                chunk = chunk * 2.0
            if kz < 16:
                out_ref[kz, group] = chunk.astype(BF16)
            else:
                for block, extra in enumerate(spread_last(chunk, 16)):
                    whole = out_ref[block, group].astype(F32) + extra
                    out_ref[block, group] = whole.astype(BF16)


def from_z_kernel(scale, data_ref, table_ref, out_ref):
    blocks = []
    for group in range(4):
        data = data_ref[:, group].astype(F32)
        for block in range(2):
            rows = data[:, block * 8 : block * 8 + 8, :].reshape(128, 128)
            last = gather_last(rows[0:8], rows[8:16], 8)
            blocks.append(jnp.concatenate([rows, last], 0).astype(BF16))
    products = dot_tn(jnp.concatenate(blocks, 1), table_ref[...])
    for group in range(4):
        first_row = (group // 2 * 76 + group % 2 * HALF) * 4
        for block in range(2):
            first = (group * 2 + block) * 128
            re = products[first : first + HALF, :256]
            im = products[first + 64 : first + 64 + HALF, 256:]
            total = (re + im) * scale
            for part in range(2):
                start = first_row + block * 2 + part
                out_ref[pl.ds(start, HALF, stride=4), :] = total[:, part * 128 : part * 128 + 128]


def vmem(count):
    return [pl.BlockSpec(memory_space=pltpu.VMEM)] * count


def grant(mib):
    return pltpu.CompilerParams(vmem_limit_bytes=mib * 2**20)


def local_call(kernel, name, result, scratch, *operands):
    return pl.pallas_call(
        kernel,
        out_shape=result,
        in_specs=vmem(len(operands)),
        out_specs=pl.BlockSpec(memory_space=pltpu.VMEM),
        scratch_shapes=[pltpu.VMEM(shape, F32) for shape in scratch],
        compiler_params=grant(8),
        name=name,
    )(*operands)


def chunks_of(*shape):
    return jax.ShapeDtypeStruct(shape, BF16)


def frequencies(spectrum, kernel):
    return pl.pallas_call(
        frequency_kernel,
        out_shape=jax.ShapeDtypeStruct((16, 4, 16, 128), BF16),
        in_specs=vmem(1) + [pl.BlockSpec(memory_space=pltpu.HBM)],
        out_specs=pl.BlockSpec(memory_space=pltpu.VMEM),
        scratch_shapes=[
            pltpu.VMEM((1216, 256), BF16),
            pltpu.VMEM((KZ, 2, 76, 16, 152), BF16),
            pltpu.VMEM((KZ, 64, 512), BF16),
            pltpu.VMEM((KZ, 64, 1216), BF16),
            pltpu.VMEM((2048, 128), F32),
            pltpu.VMEM((ROWS, 768, 128), F32),
            pltpu.SemaphoreType.DMA((KZ,)),
        ],
        compiler_params=grant(40),
        name="frequencies",
    )(spectrum, kernel)


def from_z(data, table, scale):
    return pl.pallas_call(
        functools.partial(from_z_kernel, scale),
        out_shape=jax.ShapeDtypeStruct((608, 128), F32),
        in_specs=vmem(2),
        out_specs=pl.BlockSpec(memory_space=pltpu.VMEM),
        compiler_params=grant(8),
        name="from_z",
    )(data, table)


def exchange(chunks, axes):
    return lax.all_to_all(chunks, axes, 0, 0, tiled=True)


def on_device(multipoles, kernel):
    near = ("bx", "by")
    plane = (1024, 128)
    field = multipoles[:, :, 0, :].transpose(1, 0, 2)
    rows = local_call(
        spread_rows_kernel, "spread_rows", chunks_of(64, 16, 128), [(4, 168, 128), plane], field
    )
    rows = exchange(rows, near)
    spectrum = local_call(
        to_waves_kernel, "to_waves", chunks_of(64, 2, 16, 128), [plane, plane, plane], rows
    )
    spectrum = exchange(spectrum.reshape(128, 16, 128), ("bx", "by", "col"))
    local = frequencies(spectrum, kernel.transpose(0, 1, 3, 4, 2, 5))
    local = exchange(local.reshape(64, 16, 128), near)
    back = local_call(
        from_waves_kernel, "from_waves", chunks_of(64, 1, 16, 128), [plane, plane], local
    )
    back = exchange(back.reshape(64, 16, 128), near)
    behind = jnp.asarray(table_back())
    result = from_z(back.reshape(16, 4, 16, 128), behind, 1.0 / (32 * SCALE))
    return result.reshape(multipoles.shape)


def solution(mesh):
    placed = (P(None, "col", "bx", "by"), P(None, "bx", "by", None, "col", None))
    return jax.shard_map(
        on_device, mesh=mesh, in_specs=placed, out_specs=P(None, "col", "bx", "by"), check_vma=False
    )
```

```python
import functools
import math

import jax
import jax.numpy as jnp
import numpy as np
from jax import lax
from jax.experimental import pallas as pl
from jax.experimental.pallas import tpu as pltpu
from jax.sharding import PartitionSpec as P

NB = 32
KZ = 17
RHS = 2
HALF = 38
SPARE = 19
ROWS = 3
F32 = jnp.float32
BF16 = jnp.bfloat16


def to_bf16(values):
    return np.asarray(values, np.float32).astype(jnp.bfloat16)


def table_scale():
    level = np.cos(2 * np.pi * np.arange(8) / 32)
    weight = np.array([2.0] + [4.0] * 7)
    scales = np.linspace(1.0, 2.0, 20001)[:-1]
    scaled = scales[:, None] * level[None, :]
    error = to_bf16(scaled).astype(np.float64) / scales[:, None] - level[None, :]
    return float(scales[np.argmin((weight * error**2).sum(1))])


SCALE = table_scale()


def table_back():
    kz = np.arange(KZ)[:, None]
    z = np.arange(NB)[None, :]
    angle = 2 * np.pi * ((kz * z) % NB) / NB
    eye = np.eye(8)
    cos = np.einsum("kz,ab->kabz", np.cos(angle), eye).reshape(KZ * 8, 8 * NB)
    sin = np.einsum("kz,ab->kabz", -np.sin(angle), eye).reshape(KZ * 8, 8 * NB)
    sin[128:] = 0
    return to_bf16(SCALE * np.concatenate([cos, sin], 1))


def iota(shape, axis):
    return lax.broadcasted_iota(jnp.int32, shape, axis)


def cosine(steps):
    return SCALE * jnp.cos((steps % NB).astype(F32) * (2 * math.pi / NB))


def high_part(values):
    return values.astype(BF16).astype(F32)


def line_table():
    row, lane = iota((64, 128), 0), iota((64, 128), 1)
    values = cosine((row % NB) * (lane % NB) - 8 * (row // NB))
    high = high_part(values)
    return jnp.where(lane // NB == 1, values - high, high).astype(BF16)


def ahead_table():
    row, lane = iota((128, 128), 0), iota((128, 128), 1)
    place = lane % 64
    own = (place < ROWS * KZ) & (place // KZ == row // NB)
    values = jnp.where(own, cosine((place % KZ) * (row % NB) + 8 * (lane // 64)), 0.0)
    high = high_part(values)
    return high.astype(BF16), (values - high).astype(BF16)


def select_in():
    line, lane = iota((128 * ROWS, 512), 0), iota((128 * ROWS, 512), 1)
    source = line % 128
    row = source // 2 * ROWS + line // 128
    target = row // 76 * 256 + source % 2 * 76 + row % 76
    return jnp.where((row < 152) & (lane == target), 1.0, 0.0).astype(BF16)


def pick_table():
    line, lane = iota((144, 128), 0), iota((144, 128), 1)
    block, kz = line // 24, line % 24
    return jnp.where((kz < KZ) & (lane == block % 2 * 64 + block // 2 * KZ + kz), 1.0, 0.0).astype(
        BF16
    )


def select_out():
    coefficient, lane = iota((1216, 256), 0) // 16, iota((1216, 256), 1)
    target = jnp.where(coefficient < HALF, coefficient, coefficient + 128 - HALF)
    return jnp.where(lane == target, 1.0, 0.0).astype(BF16)


def lane_index(rows):
    return lax.broadcasted_iota(jnp.int32, (rows, 128), 1)


def lanes_between(rows, low, high):
    lane = lane_index(rows) % 64
    return (lane >= low) & (lane < high)


def dot_nt(left, right):
    return lax.dot_general(left, right, (((1,), (1,)), ((), ())), preferred_element_type=F32)


def dot_tn(left, right):
    return lax.dot_general(left, right, (((0,), (0,)), ((), ())), preferred_element_type=F32)


def dot(left, right):
    return jnp.dot(left, right, preferred_element_type=F32)


def spread_last(last, rows, base=0):
    spare = lanes_between(rows, HALF, HALF + SPARE)
    first = jnp.where(spare, pltpu.roll(last, (HALF - base) % 128, 1), 0.0)
    second = jnp.where(spare, pltpu.roll(last, (HALF - SPARE - base) % 128, 1), 0.0)
    return first, second


def gather_last(first, second, rows):
    first = jnp.where(lanes_between(rows, 0, SPARE), pltpu.roll(first, 128 - HALF, 1), 0.0)
    second = jnp.where(
        lanes_between(rows, SPARE, HALF), pltpu.roll(second, 128 - HALF + SPARE, 1), 0.0
    )
    return first + second


def spread_rows_kernel(field_ref, out_ref, rows_ref, chunk_ref):
    field = field_ref[...].astype(F32)
    rows_ref[:, 152:168, :] = jnp.zeros((4, 16, 128), F32)
    for tile in range(4):
        for rhs in range(RHS):
            part = field[:, rhs, tile * 128 : tile * 128 + 128]
            rows_ref[tile, rhs * 76 : rhs * 76 + 76, :] = part
    slot = lane_index(56) // NB
    for tile in range(4):
        parts = [rows_ref[tile, pl.ds(row, 56, stride=ROWS), :] for row in range(ROWS)]
        for y in range(4):
            total = jnp.zeros((56, 128), F32)
            for row in range(ROWS):
                shift = (row - y) % 4 * NB
                moved = pltpu.roll(parts[row], shift, 1) if shift else parts[row]
                total = jnp.where(slot == row, moved, total)
            chunk_ref[pl.ds(tile * 4 + y, 56, stride=24), :] = total
    for owner in range(56):
        out_ref[owner] = chunk_ref[owner * 24 : owner * 24 + 16, :].astype(BF16)
    out_ref[56:64] = jnp.zeros((8, 16, 128), BF16)


def line_waves(table, pair, sign):
    both = jnp.concatenate(pair, 1)
    high = both.astype(BF16)
    if both.dtype == BF16:
        stacked = jnp.concatenate([high, high], 0)
    else:
        low = (both - high.astype(F32)).astype(BF16)
        stacked = jnp.concatenate([high, high, low], 0)
    product = dot(table[:, : stacked.shape[0]], stacked)
    upper = lane_index(32) < 64
    result = []
    for lane in (0, 128):
        crossed = pltpu.roll(product[32:, lane : lane + 128], 64, 1)
        result.append(
            product[:32, lane : lane + 128] + jnp.where(upper, sign * crossed, -sign * crossed)
        )
    return result


def turned(values, steps, sign, lower):
    if steps == 0:
        return values
    cos = math.cos(2 * math.pi * steps / NB)
    sin = sign * math.sin(2 * math.pi * steps / NB)
    crossed = pltpu.roll(values, 64, 1) * jnp.where(lower, sin, -sin).astype(F32)
    return crossed if steps == 8 else values * cos + crossed


def short_waves(blocks, sign, lower):
    count = len(blocks)
    if count == 1:
        return blocks
    even = short_waves(blocks[0::2], sign, lower)
    odd = short_waves(blocks[1::2], sign, lower)
    odd = [turned(odd[k], k * (NB // count), sign, lower) for k in range(count // 2)]
    return [e + o for e, o in zip(even, odd)] + [e - o for e, o in zip(even, odd)]


def plane_waves(sign, scale, copies, load, out_ref, middle_ref, end_ref):
    table = line_table()
    for x in range(0, NB, 2):
        pair = [load(i) for i in (x, x + 1)]
        for i, rows in enumerate(line_waves(table, pair, sign)):
            middle_ref[(x + i) * 32 : (x + i + 1) * 32, :] = rows
    lower = lane_index(8) < 64

    def column(place, carry):
        start = place * 8
        blocks = [middle_ref[pl.ds(start + x * 32, 8), :] for x in range(NB)]
        for x, block in enumerate(short_waves(blocks, sign, lower)):
            end_ref[pl.ds(start + x * 32, 8), :] = block
        return carry

    for place in range(4):
        column(place, 0)
    total = (end_ref[...] * scale).astype(BF16).reshape(64, 16, 128)
    for copy in range(copies):
        out_ref[:, copy] = total


def to_waves_kernel(data_ref, out_ref, start_ref, middle_ref, end_ref):
    high, low = ahead_table()
    data = data_ref[...].reshape(1024, 128)
    start_ref[...] = dot(jnp.concatenate([data, data], 1), jnp.concatenate([high, low], 0))

    def load(x):
        return start_ref[x * 32 : x * 32 + 32, :]

    plane_waves(1.0, 1.0 / SCALE**2, 2, load, out_ref, middle_ref, end_ref)


def from_waves_kernel(data_ref, out_ref, middle_ref, end_ref):
    def load(x):
        return data_ref[2 * x : 2 * x + 2].reshape(32, 128)

    plane_waves(-1.0, 1.0 / (1024 * SCALE), 1, load, out_ref, middle_ref, end_ref)


def panels(spec_ref, panel_ref, flat_ref, line_ref):
    for source in range(128):
        flat_ref[source * 24 : source * 24 + 16, :] = spec_ref[source].astype(F32)
    pick = pick_table()
    for ky in range(0, 16, 2):
        both = [flat_ref[pl.ds(i, 128, stride=24), :] for i in (ky, ky + 1)]
        turned = dot_nt(pick, jnp.concatenate(both, 0).astype(BF16))
        for i in range(2):
            for row in range(ROWS):
                for part in range(2):
                    block = turned[(row * 2 + part) * 24 : (row * 2 + part) * 24 + 24]
                    place = pl.ds(part * 16 + ky + i, 24, stride=40)
                    line_ref[row, place, :] = block[:, i * 128 : i * 128 + 128]
    lines = []
    for row in range(ROWS):
        blocks = [line_ref[row, kz * 40 : kz * 40 + 32, :].astype(BF16) for kz in range(KZ)]
        lines.append(jnp.concatenate(blocks, 0))
    total = dot(jnp.concatenate(lines, 1), select_in()).astype(BF16)
    for kz in range(KZ):
        re = total[kz * 32 : kz * 32 + 16]
        im = total[kz * 32 + 16 : kz * 32 + 32]
        for rhs in range(RHS):
            lanes = slice(rhs * 256, rhs * 256 + 256)
            upper = slice(rhs * 16, rhs * 16 + 16)
            lower = slice(32 + rhs * 16, 48 + rhs * 16)
            panel_ref[kz, upper, 0:256] = re[:, lanes]
            panel_ref[kz, lower, 0:256] = im[:, lanes]
            panel_ref[kz, upper, 256:512] = -im[:, lanes]
            panel_ref[kz, lower, 256:512] = re[:, lanes]


def frequency_kernel(
    spec_ref,
    kernel_hbm,
    out_ref,
    back_ref,
    kernel_ref,
    panel_ref,
    own_ref,
    flat_ref,
    line_ref,
    kernel_sem,
):
    def load(kz):
        return pltpu.make_async_copy(
            kernel_hbm.at[:, 0, kz], kernel_ref.at[kz], kernel_sem.at[kz]
        )

    for kz in range(KZ):
        load(kz).start()
    panels(spec_ref, panel_ref, flat_ref, line_ref)
    back_ref[...] = select_out()

    row = lax.broadcasted_iota(jnp.int32, (64, 128), 0)
    lane = lax.broadcasted_iota(jnp.int32, (64, 128), 1)
    same = row % 16 == lane % 16

    def step(kz):
        panel = panel_ref[kz]
        product = dot_nt(panel[:, 0:152], kernel_ref[kz, 0].reshape(1216, 152))
        product += dot_nt(panel[:, 256:408], kernel_ref[kz, 1].reshape(1216, 152))
        for tile in range(0, 1216, 128):
            wide = min(128, 1216 - tile)
            part = jnp.where(same[:, :wide], product[:, tile : tile + wide], 0.0)
            own_ref[kz, :, tile : tile + wide] = part.astype(BF16)

    def pair(half, carry):
        for kz in (2 * half, 2 * half + 1):
            load(kz).wait()
        for kz in (2 * half, 2 * half + 1):
            step(kz)
        return carry

    lax.fori_loop(0, KZ // 2, pair, 0)
    load(KZ - 1).wait()
    step(KZ - 1)

    local = dot(own_ref[...].reshape(KZ * 64, 1216), back_ref[...]).reshape(KZ, 64, 256)
    for kz in range(KZ):
        for group in range(4):
            rhs, half = group // 2, group % 2
            tile = local[kz, :, half * 128 : half * 128 + 128]
            im = pltpu.roll(tile[32 + rhs * 16 : 48 + rhs * 16], 64, 1)
            chunk = tile[rhs * 16 : rhs * 16 + 16] + im
            if kz not in (0, 16):
                chunk = chunk * 2.0
            if kz < 16:
                out_ref[kz, group] = chunk.astype(BF16)
            else:
                for block, extra in enumerate(spread_last(chunk, 16)):
                    whole = out_ref[block, group].astype(F32) + extra
                    out_ref[block, group] = whole.astype(BF16)


def from_z_kernel(scale, data_ref, table_ref, out_ref):
    blocks = []
    for group in range(4):
        data = data_ref[:, group].astype(F32)
        for block in range(2):
            rows = data[:, block * 8 : block * 8 + 8, :].reshape(128, 128)
            last = gather_last(rows[0:8], rows[8:16], 8)
            blocks.append(jnp.concatenate([rows, last], 0).astype(BF16))
    products = dot_tn(jnp.concatenate(blocks, 1), table_ref[...])
    for group in range(4):
        first_row = (group // 2 * 76 + group % 2 * HALF) * 4
        for block in range(2):
            first = (group * 2 + block) * 128
            re = products[first : first + HALF, :256]
            im = products[first + 64 : first + 64 + HALF, 256:]
            total = (re + im) * scale
            for part in range(2):
                start = first_row + block * 2 + part
                out_ref[pl.ds(start, HALF, stride=4), :] = total[:, part * 128 : part * 128 + 128]


def vmem(count):
    return [pl.BlockSpec(memory_space=pltpu.VMEM)] * count


def grant(mib):
    return pltpu.CompilerParams(vmem_limit_bytes=mib * 2**20)


def local_call(kernel, name, result, scratch, *operands):
    return pl.pallas_call(
        kernel,
        out_shape=result,
        in_specs=vmem(len(operands)),
        out_specs=pl.BlockSpec(memory_space=pltpu.VMEM),
        scratch_shapes=[pltpu.VMEM(shape, F32) for shape in scratch],
        compiler_params=grant(8),
        name=name,
    )(*operands)


def chunks_of(*shape):
    return jax.ShapeDtypeStruct(shape, BF16)


def frequencies(spectrum, kernel):
    return pl.pallas_call(
        frequency_kernel,
        out_shape=jax.ShapeDtypeStruct((16, 4, 16, 128), BF16),
        in_specs=vmem(1) + [pl.BlockSpec(memory_space=pltpu.HBM)],
        out_specs=pl.BlockSpec(memory_space=pltpu.VMEM),
        scratch_shapes=[
            pltpu.VMEM((1216, 256), BF16),
            pltpu.VMEM((KZ, 2, 76, 16, 152), BF16),
            pltpu.VMEM((KZ, 64, 512), BF16),
            pltpu.VMEM((KZ, 64, 1216), BF16),
            pltpu.VMEM((3072, 128), F32),
            pltpu.VMEM((ROWS, 960, 128), F32),
            pltpu.SemaphoreType.DMA((KZ,)),
        ],
        compiler_params=grant(40),
        name="frequencies",
    )(spectrum, kernel)


def from_z(data, table, scale):
    return pl.pallas_call(
        functools.partial(from_z_kernel, scale),
        out_shape=jax.ShapeDtypeStruct((608, 128), F32),
        in_specs=vmem(2),
        out_specs=pl.BlockSpec(memory_space=pltpu.VMEM),
        compiler_params=grant(8),
        name="from_z",
    )(data, table)


def exchange(chunks, axes):
    return lax.all_to_all(chunks, axes, 0, 0, tiled=True)


def on_device(multipoles, kernel):
    near = ("bx", "by")
    plane = (1024, 128)
    field = multipoles[:, :, 0, :].transpose(1, 0, 2)
    rows = local_call(
        spread_rows_kernel, "spread_rows", chunks_of(64, 16, 128), [(4, 168, 128), (1344, 128)], field
    )
    rows = exchange(rows, near)
    spectrum = local_call(
        to_waves_kernel, "to_waves", chunks_of(64, 2, 16, 128), [plane, plane, plane], rows
    )
    spectrum = exchange(spectrum.reshape(128, 16, 128), ("bx", "by", "col"))
    local = frequencies(spectrum, kernel.transpose(0, 1, 3, 4, 2, 5))
    local = exchange(local.reshape(64, 16, 128), near)
    back = local_call(
        from_waves_kernel, "from_waves", chunks_of(64, 1, 16, 128), [plane, plane], local
    )
    back = exchange(back.reshape(64, 16, 128), near)
    behind = jnp.asarray(table_back())
    result = from_z(back.reshape(16, 4, 16, 128), behind, 1.0 / (32 * SCALE))
    return result.reshape(multipoles.shape)


def solution(mesh):
    placed = (P(None, "col", "bx", "by"), P(None, "bx", "by", None, "col", None))
    return jax.shard_map(
        on_device, mesh=mesh, in_specs=placed, out_specs=P(None, "col", "bx", "by"), check_vma=False
    )
```

```python
import functools
import math

import jax
import jax.numpy as jnp
import numpy as np
from jax import lax
from jax.experimental import pallas as pl
from jax.experimental.pallas import tpu as pltpu
from jax.sharding import PartitionSpec as P

NB = 32
KZ = 17
RHS = 2
HALF = 38
SPARE = 19
ROWS = 3
HEAD = 3
F32 = jnp.float32
BF16 = jnp.bfloat16


def to_bf16(values):
    return np.asarray(values, np.float32).astype(jnp.bfloat16)


def table_scale():
    level = np.cos(2 * np.pi * np.arange(8) / 32)
    weight = np.array([2.0] + [4.0] * 7)
    scales = np.linspace(1.0, 2.0, 20001)[:-1]
    scaled = scales[:, None] * level[None, :]
    error = to_bf16(scaled).astype(np.float64) / scales[:, None] - level[None, :]
    return float(scales[np.argmin((weight * error**2).sum(1))])


SCALE = table_scale()


def table_back():
    kz = np.arange(KZ)[:, None]
    z = np.arange(NB)[None, :]
    angle = 2 * np.pi * ((kz * z) % NB) / NB
    eye = np.eye(8)
    cos = np.einsum("kz,ab->kabz", np.cos(angle), eye).reshape(KZ * 8, 8 * NB)
    sin = np.einsum("kz,ab->kabz", -np.sin(angle), eye).reshape(KZ * 8, 8 * NB)
    sin[128:] = 0
    return to_bf16(SCALE * np.concatenate([cos, sin], 1))


def iota(shape, axis):
    return lax.broadcasted_iota(jnp.int32, shape, axis)


def cosine(steps):
    return SCALE * jnp.cos((steps % NB).astype(F32) * (2 * math.pi / NB))


def high_part(values):
    return values.astype(BF16).astype(F32)


def line_table():
    row, lane = iota((64, 128), 0), iota((64, 128), 1)
    values = cosine((row % NB) * (lane % NB) - 8 * (row // NB))
    high = high_part(values)
    return jnp.where(lane // NB == 1, values - high, high).astype(BF16)


def ahead_table():
    row, lane = iota((128, 128), 0), iota((128, 128), 1)
    place = lane % 64
    own = (place < ROWS * KZ) & (place // KZ == row // NB)
    values = jnp.where(own, cosine((place % KZ) * (row % NB) + 8 * (lane // 64)), 0.0)
    high = high_part(values)
    return high.astype(BF16), (values - high).astype(BF16)


def select_in():
    line, lane = iota((128 * ROWS, 512), 0), iota((128 * ROWS, 512), 1)
    source = line % 128
    row = source // 2 * ROWS + line // 128
    target = row // 76 * 256 + source % 2 * 76 + row % 76
    return jnp.where((row < 152) & (lane == target), 1.0, 0.0).astype(BF16)


def pick_table():
    line, lane = iota((144, 128), 0), iota((144, 128), 1)
    block, kz = line // 24, line % 24
    return jnp.where((kz < KZ) & (lane == block % 2 * 64 + block // 2 * KZ + kz), 1.0, 0.0).astype(
        BF16
    )


def select_out():
    coefficient, lane = iota((1216, 256), 0) // 16, iota((1216, 256), 1)
    target = jnp.where(coefficient < HALF, coefficient, coefficient + 128 - HALF)
    return jnp.where(lane == target, 1.0, 0.0).astype(BF16)


def lane_index(rows):
    return lax.broadcasted_iota(jnp.int32, (rows, 128), 1)


def lanes_between(rows, low, high):
    lane = lane_index(rows) % 64
    return (lane >= low) & (lane < high)


def dot_nt(left, right):
    return lax.dot_general(left, right, (((1,), (1,)), ((), ())), preferred_element_type=F32)


def dot_tn(left, right):
    return lax.dot_general(left, right, (((0,), (0,)), ((), ())), preferred_element_type=F32)


def dot(left, right):
    return jnp.dot(left, right, preferred_element_type=F32)


def spread_last(last, rows, base=0):
    spare = lanes_between(rows, HALF, HALF + SPARE)
    first = jnp.where(spare, pltpu.roll(last, (HALF - base) % 128, 1), 0.0)
    second = jnp.where(spare, pltpu.roll(last, (HALF - SPARE - base) % 128, 1), 0.0)
    return first, second


def gather_last(first, second, rows):
    first = jnp.where(lanes_between(rows, 0, SPARE), pltpu.roll(first, 128 - HALF, 1), 0.0)
    second = jnp.where(
        lanes_between(rows, SPARE, HALF), pltpu.roll(second, 128 - HALF + SPARE, 1), 0.0
    )
    return first + second


def spread_rows_kernel(field_ref, out_ref, rows_ref, chunk_ref):
    field = field_ref[...].astype(F32)
    rows_ref[:, 152:168, :] = jnp.zeros((4, 16, 128), F32)
    for tile in range(4):
        for rhs in range(RHS):
            part = field[:, rhs, tile * 128 : tile * 128 + 128]
            rows_ref[tile, rhs * 76 : rhs * 76 + 76, :] = part
    slot = lane_index(56) // NB
    for tile in range(4):
        parts = [rows_ref[tile, pl.ds(row, 56, stride=ROWS), :] for row in range(ROWS)]
        for y in range(4):
            total = jnp.zeros((56, 128), F32)
            for row in range(ROWS):
                shift = (row - y) % 4 * NB
                moved = pltpu.roll(parts[row], shift, 1) if shift else parts[row]
                total = jnp.where(slot == row, moved, total)
            chunk_ref[pl.ds(tile * 4 + y, 56, stride=24), :] = total
    for owner in range(56):
        out_ref[owner] = chunk_ref[owner * 24 : owner * 24 + 16, :].astype(BF16)
    out_ref[56:64] = jnp.zeros((8, 16, 128), BF16)


def line_waves(table, pair, sign):
    both = jnp.concatenate(pair, 1)
    high = both.astype(BF16)
    if both.dtype == BF16:
        stacked = jnp.concatenate([high, high], 0)
    else:
        low = (both - high.astype(F32)).astype(BF16)
        stacked = jnp.concatenate([high, high, low], 0)
    product = dot(table[:, : stacked.shape[0]], stacked)
    upper = lane_index(32) < 64
    result = []
    for lane in (0, 128):
        crossed = pltpu.roll(product[32:, lane : lane + 128], 64, 1)
        result.append(
            product[:32, lane : lane + 128] + jnp.where(upper, sign * crossed, -sign * crossed)
        )
    return result


def turned(values, steps, sign, lower):
    if steps == 0:
        return values
    cos = math.cos(2 * math.pi * steps / NB)
    sin = sign * math.sin(2 * math.pi * steps / NB)
    crossed = pltpu.roll(values, 64, 1) * jnp.where(lower, sin, -sin).astype(F32)
    return crossed if steps == 8 else values * cos + crossed


def short_waves(blocks, sign, lower):
    count = len(blocks)
    if count == 1:
        return blocks
    even = short_waves(blocks[0::2], sign, lower)
    odd = short_waves(blocks[1::2], sign, lower)
    odd = [turned(odd[k], k * (NB // count), sign, lower) for k in range(count // 2)]
    return [e + o for e, o in zip(even, odd)] + [e - o for e, o in zip(even, odd)]


def plane_waves(sign, scale, copies, load, out_ref, middle_ref, end_ref):
    table = line_table()
    for x in range(0, NB, 2):
        pair = [load(i) for i in (x, x + 1)]
        for i, rows in enumerate(line_waves(table, pair, sign)):
            middle_ref[(x + i) * 32 : (x + i + 1) * 32, :] = rows
    lower = lane_index(8) < 64

    def column(place, carry):
        start = place * 8
        blocks = [middle_ref[pl.ds(start + x * 32, 8), :] for x in range(NB)]
        for x, block in enumerate(short_waves(blocks, sign, lower)):
            end_ref[pl.ds(start + x * 32, 8), :] = block
        return carry

    for place in range(4):
        column(place, 0)
    total = (end_ref[...] * scale).astype(BF16).reshape(64, 16, 128)
    for copy in range(copies):
        out_ref[:, copy] = total


def kernel_copy(kernel_hbm, target_ref, sem, kz, place):
    return pltpu.make_async_copy(kernel_hbm.at[:, 0, kz], target_ref.at[place], sem.at[place])


def to_waves_kernel(
    data_ref, kernel_hbm, out_ref, head_ref, start_ref, middle_ref, end_ref, head_sem
):
    copies = [kernel_copy(kernel_hbm, head_ref, head_sem, kz, kz) for kz in range(HEAD)]
    for copy in copies:
        copy.start()
    high, low = ahead_table()
    data = data_ref[...].reshape(1024, 128)
    start_ref[...] = dot(jnp.concatenate([data, data], 1), jnp.concatenate([high, low], 0))

    def load(x):
        return start_ref[x * 32 : x * 32 + 32, :]

    plane_waves(1.0, 1.0 / SCALE**2, 2, load, out_ref, middle_ref, end_ref)
    for copy in copies:
        copy.wait()


def from_waves_kernel(data_ref, out_ref, middle_ref, end_ref):
    def load(x):
        return data_ref[2 * x : 2 * x + 2].reshape(32, 128)

    plane_waves(-1.0, 1.0 / (1024 * SCALE), 1, load, out_ref, middle_ref, end_ref)


def panels(spec_ref, panel_ref, flat_ref, line_ref):
    for source in range(128):
        flat_ref[source * 24 : source * 24 + 16, :] = spec_ref[source].astype(F32)
    pick = pick_table()
    for ky in range(0, 16, 2):
        both = [flat_ref[pl.ds(i, 128, stride=24), :] for i in (ky, ky + 1)]
        turned = dot_nt(pick, jnp.concatenate(both, 0).astype(BF16))
        for i in range(2):
            for row in range(ROWS):
                for part in range(2):
                    block = turned[(row * 2 + part) * 24 : (row * 2 + part) * 24 + 24]
                    place = pl.ds(part * 16 + ky + i, 24, stride=40)
                    line_ref[row, place, :] = block[:, i * 128 : i * 128 + 128]
    lines = []
    for row in range(ROWS):
        blocks = [line_ref[row, kz * 40 : kz * 40 + 32, :].astype(BF16) for kz in range(KZ)]
        lines.append(jnp.concatenate(blocks, 0))
    total = dot(jnp.concatenate(lines, 1), select_in()).astype(BF16)
    for kz in range(KZ):
        re = total[kz * 32 : kz * 32 + 16]
        im = total[kz * 32 + 16 : kz * 32 + 32]
        for rhs in range(RHS):
            lanes = slice(rhs * 256, rhs * 256 + 256)
            upper = slice(rhs * 16, rhs * 16 + 16)
            lower = slice(32 + rhs * 16, 48 + rhs * 16)
            panel_ref[kz, upper, 0:256] = re[:, lanes]
            panel_ref[kz, lower, 0:256] = im[:, lanes]
            panel_ref[kz, upper, 256:512] = -im[:, lanes]
            panel_ref[kz, lower, 256:512] = re[:, lanes]


def frequency_kernel(
    spec_ref,
    head_ref,
    kernel_hbm,
    out_ref,
    back_ref,
    kernel_ref,
    panel_ref,
    own_ref,
    flat_ref,
    line_ref,
    kernel_sem,
):
    def load(kz):
        return kernel_copy(kernel_hbm, kernel_ref, kernel_sem, kz, kz - HEAD)

    for kz in range(HEAD, KZ):
        load(kz).start()
    panels(spec_ref, panel_ref, flat_ref, line_ref)
    back_ref[...] = select_out()

    row = lax.broadcasted_iota(jnp.int32, (64, 128), 0)
    lane = lax.broadcasted_iota(jnp.int32, (64, 128), 1)
    same = row % 16 == lane % 16

    def step(kz, matrix_ref, place):
        panel = panel_ref[kz]
        product = dot_nt(panel[:, 0:152], matrix_ref[place, 0].reshape(1216, 152))
        product += dot_nt(panel[:, 256:408], matrix_ref[place, 1].reshape(1216, 152))
        for tile in range(0, 1216, 128):
            wide = min(128, 1216 - tile)
            part = jnp.where(same[:, :wide], product[:, tile : tile + wide], 0.0)
            own_ref[kz, :, tile : tile + wide] = part.astype(BF16)

    def ahead(kz, carry):
        step(kz, head_ref, kz)
        return carry

    def pair(half, carry):
        places = (2 * half, 2 * half + 1)
        for place in places:
            load(place + HEAD).wait()
        for place in places:
            step(place + HEAD, kernel_ref, place)
        return carry

    lax.fori_loop(0, HEAD, ahead, 0)
    lax.fori_loop(0, (KZ - HEAD) // 2, pair, 0)

    local = dot(own_ref[...].reshape(KZ * 64, 1216), back_ref[...]).reshape(KZ, 64, 256)
    for kz in range(KZ):
        for group in range(4):
            rhs, half = group // 2, group % 2
            tile = local[kz, :, half * 128 : half * 128 + 128]
            im = pltpu.roll(tile[32 + rhs * 16 : 48 + rhs * 16], 64, 1)
            chunk = tile[rhs * 16 : rhs * 16 + 16] + im
            if kz not in (0, 16):
                chunk = chunk * 2.0
            if kz < 16:
                out_ref[kz, group] = chunk.astype(BF16)
            else:
                for block, extra in enumerate(spread_last(chunk, 16)):
                    whole = out_ref[block, group].astype(F32) + extra
                    out_ref[block, group] = whole.astype(BF16)


def from_z_kernel(scale, data_ref, table_ref, out_hbm, out_ref, sem):
    copies = []
    for group in range(4):
        data = data_ref[:, group].astype(F32)
        blocks = []
        for block in range(2):
            rows = data[:, block * 8 : block * 8 + 8, :].reshape(128, 128)
            last = gather_last(rows[0:8], rows[8:16], 8)
            blocks.append(jnp.concatenate([rows, last], 0).astype(BF16))
        products = dot_tn(jnp.concatenate(blocks, 1), table_ref[...])
        first_row = group * HALF * 4
        for block in range(2):
            re = products[block * 128 : block * 128 + HALF, :256]
            im = products[block * 128 + 64 : block * 128 + 64 + HALF, 256:]
            total = (re + im) * scale
            for part in range(2):
                start = first_row + block * 2 + part
                out_ref[pl.ds(start, HALF, stride=4), :] = total[:, part * 128 : part * 128 + 128]
        rows = pl.ds(first_row, HALF * 4)
        copies.append(pltpu.make_async_copy(out_ref.at[rows], out_hbm.at[rows], sem.at[group]))
        copies[-1].start()
    for copy in copies:
        copy.wait()


def vmem(count):
    return [pl.BlockSpec(memory_space=pltpu.VMEM)] * count


def grant(mib):
    return pltpu.CompilerParams(vmem_limit_bytes=mib * 2**20)


def local_call(kernel, name, result, scratch, *operands):
    return pl.pallas_call(
        kernel,
        out_shape=result,
        in_specs=vmem(len(operands)),
        out_specs=pl.BlockSpec(memory_space=pltpu.VMEM),
        scratch_shapes=[pltpu.VMEM(shape, F32) for shape in scratch],
        compiler_params=grant(8),
        name=name,
    )(*operands)


def chunks_of(*shape):
    return jax.ShapeDtypeStruct(shape, BF16)


def to_waves(rows, kernel):
    plane = pltpu.VMEM((1024, 128), F32)
    return pl.pallas_call(
        to_waves_kernel,
        out_shape=(chunks_of(64, 2, 16, 128), chunks_of(HEAD, 2, 76, 16, 152)),
        in_specs=vmem(1) + [pl.BlockSpec(memory_space=pltpu.HBM)],
        out_specs=tuple(vmem(2)),
        scratch_shapes=[plane, plane, plane, pltpu.SemaphoreType.DMA((HEAD,))],
        compiler_params=grant(40),
        name="to_waves",
    )(rows, kernel)


def frequencies(spectrum, head, kernel):
    return pl.pallas_call(
        frequency_kernel,
        out_shape=jax.ShapeDtypeStruct((16, 4, 16, 128), BF16),
        in_specs=vmem(2) + [pl.BlockSpec(memory_space=pltpu.HBM)],
        out_specs=pl.BlockSpec(memory_space=pltpu.VMEM),
        scratch_shapes=[
            pltpu.VMEM((1216, 256), BF16),
            pltpu.VMEM((KZ - HEAD, 2, 76, 16, 152), BF16),
            pltpu.VMEM((KZ, 64, 512), BF16),
            pltpu.VMEM((KZ, 64, 1216), BF16),
            pltpu.VMEM((3072, 128), F32),
            pltpu.VMEM((ROWS, 960, 128), F32),
            pltpu.SemaphoreType.DMA((KZ - HEAD,)),
        ],
        compiler_params=grant(40),
        name="frequencies",
    )(spectrum, head, kernel)


def from_z(data, table, scale):
    return pl.pallas_call(
        functools.partial(from_z_kernel, scale),
        out_shape=jax.ShapeDtypeStruct((608, 128), F32),
        in_specs=vmem(2),
        out_specs=pl.BlockSpec(memory_space=pltpu.HBM),
        scratch_shapes=[pltpu.VMEM((608, 128), F32), pltpu.SemaphoreType.DMA((4,))],
        compiler_params=grant(8),
        name="from_z",
    )(data, table)


def exchange(chunks, axes):
    return lax.all_to_all(chunks, axes, 0, 0, tiled=True)


def on_device(multipoles, kernel):
    near = ("bx", "by")
    plane = (1024, 128)
    field = multipoles[:, :, 0, :].transpose(1, 0, 2)
    rows = local_call(
        spread_rows_kernel, "spread_rows", chunks_of(64, 16, 128), [(4, 168, 128), (1344, 128)], field
    )
    rows = exchange(rows, near)
    kernel = kernel.transpose(0, 1, 3, 4, 2, 5)
    spectrum, head = to_waves(rows, kernel)
    spectrum = exchange(spectrum.reshape(128, 16, 128), ("bx", "by", "col"))
    local = frequencies(spectrum, head, kernel)
    local = exchange(local.reshape(64, 16, 128), near)
    back = local_call(
        from_waves_kernel, "from_waves", chunks_of(64, 1, 16, 128), [plane, plane], local
    )
    back = exchange(back.reshape(64, 16, 128), near)
    behind = jnp.asarray(table_back())
    result = from_z(back.reshape(16, 4, 16, 128), behind, 1.0 / (32 * SCALE))
    return result.reshape(multipoles.shape)


def solution(mesh):
    placed = (P(None, "col", "bx", "by"), P(None, "bx", "by", None, "col", None))
    return jax.shard_map(
        on_device, mesh=mesh, in_specs=placed, out_specs=P(None, "col", "bx", "by"), check_vma=False
    )
```

```python
import functools
import math

import jax
import jax.numpy as jnp
import numpy as np
from jax import lax
from jax.experimental import pallas as pl
from jax.experimental.pallas import tpu as pltpu
from jax.sharding import PartitionSpec as P

NB = 32
KZ = 17
RHS = 2
HALF = 38
SPARE = 19
ROWS = 3
F32 = jnp.float32
BF16 = jnp.bfloat16


def to_bf16(values):
    return np.asarray(values, np.float32).astype(jnp.bfloat16)


def table_scale():
    level = np.cos(2 * np.pi * np.arange(8) / 32)
    weight = np.array([2.0] + [4.0] * 7)
    scales = np.linspace(1.0, 2.0, 20001)[:-1]
    scaled = scales[:, None] * level[None, :]
    error = to_bf16(scaled).astype(np.float64) / scales[:, None] - level[None, :]
    return float(scales[np.argmin((weight * error**2).sum(1))])


SCALE = table_scale()


def table_back():
    kz = np.arange(KZ)[:, None]
    z = np.arange(NB)[None, :]
    angle = 2 * np.pi * ((kz * z) % NB) / NB
    eye = np.eye(8)
    cos = np.einsum("kz,ab->kabz", np.cos(angle), eye).reshape(KZ * 8, 8 * NB)
    sin = np.einsum("kz,ab->kabz", -np.sin(angle), eye).reshape(KZ * 8, 8 * NB)
    sin[128:] = 0
    return to_bf16(SCALE * np.concatenate([cos, sin], 1))


def iota(shape, axis):
    return lax.broadcasted_iota(jnp.int32, shape, axis)


def cosine(steps):
    return SCALE * jnp.cos((steps % NB).astype(F32) * (2 * math.pi / NB))


def high_part(values):
    return values.astype(BF16).astype(F32)


def line_table():
    row, lane = iota((64, 128), 0), iota((64, 128), 1)
    values = cosine((row % NB) * (lane % NB) - 8 * (row // NB))
    high = high_part(values)
    return jnp.where(lane // NB == 1, values - high, high).astype(BF16)


def ahead_table():
    row, lane = iota((128, 128), 0), iota((128, 128), 1)
    place = lane % 64
    own = (place < ROWS * KZ) & (place // KZ == row // NB)
    values = jnp.where(own, cosine((place % KZ) * (row % NB) + 8 * (lane // 64)), 0.0)
    high = high_part(values)
    return high.astype(BF16), (values - high).astype(BF16)


def select_in():
    line, lane = iota((128 * ROWS, 512), 0), iota((128 * ROWS, 512), 1)
    source = line % 128
    row = source // 2 * ROWS + line // 128
    target = row // 76 * 256 + source % 2 * 76 + row % 76
    return jnp.where((row < 152) & (lane == target), 1.0, 0.0).astype(BF16)


def pick_table():
    line, lane = iota((144, 128), 0), iota((144, 128), 1)
    block, kz = line // 24, line % 24
    return jnp.where((kz < KZ) & (lane == block % 2 * 64 + block // 2 * KZ + kz), 1.0, 0.0).astype(
        BF16
    )


def select_out():
    coefficient, lane = iota((1216, 256), 0) // 16, iota((1216, 256), 1)
    target = jnp.where(coefficient < HALF, coefficient, coefficient + 128 - HALF)
    return jnp.where(lane == target, 1.0, 0.0).astype(BF16)


def lane_index(rows):
    return lax.broadcasted_iota(jnp.int32, (rows, 128), 1)


def lanes_between(rows, low, high):
    lane = lane_index(rows) % 64
    return (lane >= low) & (lane < high)


def dot_nt(left, right):
    return lax.dot_general(left, right, (((1,), (1,)), ((), ())), preferred_element_type=F32)


def dot_tn(left, right):
    return lax.dot_general(left, right, (((0,), (0,)), ((), ())), preferred_element_type=F32)


def dot(left, right):
    return jnp.dot(left, right, preferred_element_type=F32)


def spread_last(last, rows, base=0):
    spare = lanes_between(rows, HALF, HALF + SPARE)
    first = jnp.where(spare, pltpu.roll(last, (HALF - base) % 128, 1), 0.0)
    second = jnp.where(spare, pltpu.roll(last, (HALF - SPARE - base) % 128, 1), 0.0)
    return first, second


def gather_last(first, second, rows):
    first = jnp.where(lanes_between(rows, 0, SPARE), pltpu.roll(first, 128 - HALF, 1), 0.0)
    second = jnp.where(
        lanes_between(rows, SPARE, HALF), pltpu.roll(second, 128 - HALF + SPARE, 1), 0.0
    )
    return first + second


def spread_rows_kernel(field_ref, out_ref, rows_ref, chunk_ref):
    field = field_ref[...].astype(F32)
    rows_ref[:, 152:168, :] = jnp.zeros((4, 16, 128), F32)
    for tile in range(4):
        for rhs in range(RHS):
            part = field[:, rhs, tile * 128 : tile * 128 + 128]
            rows_ref[tile, rhs * 76 : rhs * 76 + 76, :] = part
    slot = lane_index(56) // NB
    for tile in range(4):
        parts = [rows_ref[tile, pl.ds(row, 56, stride=ROWS), :] for row in range(ROWS)]
        for y in range(4):
            total = jnp.zeros((56, 128), F32)
            for row in range(ROWS):
                shift = (row - y) % 4 * NB
                moved = pltpu.roll(parts[row], shift, 1) if shift else parts[row]
                total = jnp.where(slot == row, moved, total)
            chunk_ref[pl.ds(tile * 4 + y, 56, stride=24), :] = total
    for owner in range(56):
        out_ref[owner] = chunk_ref[owner * 24 : owner * 24 + 16, :].astype(BF16)
    out_ref[56:64] = jnp.zeros((8, 16, 128), BF16)


def line_waves(table, pair, sign):
    both = jnp.concatenate(pair, 1)
    high = both.astype(BF16)
    if both.dtype == BF16:
        stacked = jnp.concatenate([high, high], 0)
    else:
        low = (both - high.astype(F32)).astype(BF16)
        stacked = jnp.concatenate([high, high, low], 0)
    product = dot(table[:, : stacked.shape[0]], stacked)
    upper = lane_index(32) < 64
    result = []
    for lane in (0, 128):
        crossed = pltpu.roll(product[32:, lane : lane + 128], 64, 1)
        result.append(
            product[:32, lane : lane + 128] + jnp.where(upper, sign * crossed, -sign * crossed)
        )
    return result


def turned(values, steps, sign, lower):
    if steps == 0:
        return values
    cos = math.cos(2 * math.pi * steps / NB)
    sin = sign * math.sin(2 * math.pi * steps / NB)
    crossed = pltpu.roll(values, 64, 1) * jnp.where(lower, sin, -sin).astype(F32)
    return crossed if steps == 8 else values * cos + crossed


def short_waves(blocks, sign, lower):
    count = len(blocks)
    if count == 1:
        return blocks
    even = short_waves(blocks[0::2], sign, lower)
    odd = short_waves(blocks[1::2], sign, lower)
    odd = [turned(odd[k], k * (NB // count), sign, lower) for k in range(count // 2)]
    return [e + o for e, o in zip(even, odd)] + [e - o for e, o in zip(even, odd)]


def plane_waves(sign, scale, copies, load, out_ref, middle_ref, end_ref):
    table = line_table()
    for x in range(0, NB, 2):
        pair = [load(i) for i in (x, x + 1)]
        for i, rows in enumerate(line_waves(table, pair, sign)):
            middle_ref[(x + i) * 32 : (x + i + 1) * 32, :] = rows
    lower = lane_index(8) < 64

    def column(place, carry):
        start = place * 8
        blocks = [middle_ref[pl.ds(start + x * 32, 8), :] for x in range(NB)]
        for x, block in enumerate(short_waves(blocks, sign, lower)):
            end_ref[pl.ds(start + x * 32, 8), :] = block
        return carry

    for place in range(4):
        column(place, 0)
    total = (end_ref[...] * scale).astype(BF16).reshape(64, 16, 128)
    for copy in range(copies):
        out_ref[:, copy] = total


def to_waves_kernel(data_ref, out_ref, start_ref, middle_ref, end_ref):
    high, low = ahead_table()
    data = data_ref[...].reshape(1024, 128)
    start_ref[...] = dot(jnp.concatenate([data, data], 1), jnp.concatenate([high, low], 0))

    def load(x):
        return start_ref[x * 32 : x * 32 + 32, :]

    plane_waves(1.0, 1.0 / SCALE**2, 2, load, out_ref, middle_ref, end_ref)


def from_waves_kernel(data_ref, out_ref, middle_ref, end_ref):
    def load(x):
        return data_ref[2 * x : 2 * x + 2].reshape(32, 128)

    plane_waves(-1.0, 1.0 / (1024 * SCALE), 1, load, out_ref, middle_ref, end_ref)


def panels(spec_ref, panel_ref, flat_ref, line_ref):
    for source in range(128):
        flat_ref[source * 24 : source * 24 + 16, :] = spec_ref[source].astype(F32)
    pick = pick_table()
    for ky in range(0, 16, 2):
        both = [flat_ref[pl.ds(i, 128, stride=24), :] for i in (ky, ky + 1)]
        turned = dot_nt(pick, jnp.concatenate(both, 0).astype(BF16))
        for i in range(2):
            for row in range(ROWS):
                for part in range(2):
                    block = turned[(row * 2 + part) * 24 : (row * 2 + part) * 24 + 24]
                    place = pl.ds(part * 16 + ky + i, 24, stride=40)
                    line_ref[row, place, :] = block[:, i * 128 : i * 128 + 128]
    lines = []
    for row in range(ROWS):
        blocks = [line_ref[row, kz * 40 : kz * 40 + 32, :].astype(BF16) for kz in range(KZ)]
        lines.append(jnp.concatenate(blocks, 0))
    total = dot(jnp.concatenate(lines, 1), select_in()).astype(BF16)
    for kz in range(KZ):
        re = total[kz * 32 : kz * 32 + 16]
        im = total[kz * 32 + 16 : kz * 32 + 32]
        for rhs in range(RHS):
            lanes = slice(rhs * 256, rhs * 256 + 256)
            upper = slice(rhs * 16, rhs * 16 + 16)
            lower = slice(32 + rhs * 16, 48 + rhs * 16)
            panel_ref[kz, upper, 0:256] = re[:, lanes]
            panel_ref[kz, lower, 0:256] = im[:, lanes]
            panel_ref[kz, upper, 256:512] = -im[:, lanes]
            panel_ref[kz, lower, 256:512] = re[:, lanes]


def frequency_kernel(
    spec_ref,
    kernel_hbm,
    out_ref,
    back_ref,
    kernel_ref,
    panel_ref,
    own_ref,
    flat_ref,
    line_ref,
    kernel_sem,
):
    def load(kz):
        return pltpu.make_async_copy(
            kernel_hbm.at[:, 0, kz], kernel_ref.at[kz], kernel_sem.at[kz]
        )

    for kz in range(KZ):
        load(kz).start()
    panels(spec_ref, panel_ref, flat_ref, line_ref)
    back_ref[...] = select_out()

    row = lax.broadcasted_iota(jnp.int32, (64, 128), 0)
    lane = lax.broadcasted_iota(jnp.int32, (64, 128), 1)
    same = row % 16 == lane % 16

    def step(kz):
        panel = panel_ref[kz]
        product = dot_nt(panel[:, 0:152], kernel_ref[kz, 0].reshape(1216, 152))
        product += dot_nt(panel[:, 256:408], kernel_ref[kz, 1].reshape(1216, 152))
        for tile in range(0, 1216, 128):
            wide = min(128, 1216 - tile)
            part = jnp.where(same[:, :wide], product[:, tile : tile + wide], 0.0)
            own_ref[kz, :, tile : tile + wide] = part.astype(BF16)

    def pair(half, carry):
        for kz in (2 * half, 2 * half + 1):
            load(kz).wait()
        for kz in (2 * half, 2 * half + 1):
            step(kz)
        return carry

    lax.fori_loop(0, KZ // 2, pair, 0)
    load(KZ - 1).wait()
    step(KZ - 1)

    local = dot(own_ref[...].reshape(KZ * 64, 1216), back_ref[...]).reshape(KZ, 64, 256)
    for kz in range(KZ):
        for group in range(4):
            rhs, half = group // 2, group % 2
            tile = local[kz, :, half * 128 : half * 128 + 128]
            im = pltpu.roll(tile[32 + rhs * 16 : 48 + rhs * 16], 64, 1)
            chunk = tile[rhs * 16 : rhs * 16 + 16] + im
            if kz not in (0, 16):
                chunk = chunk * 2.0
            if kz < 16:
                out_ref[kz, group] = chunk.astype(BF16)
            else:
                for block, extra in enumerate(spread_last(chunk, 16)):
                    whole = out_ref[block, group].astype(F32) + extra
                    out_ref[block, group] = whole.astype(BF16)


def from_z_kernel(scale, data_ref, table_ref, out_hbm, out_ref, sem):
    copies = []
    for group in range(4):
        data = data_ref[:, group].astype(F32)
        blocks = []
        for block in range(2):
            rows = data[:, block * 8 : block * 8 + 8, :].reshape(128, 128)
            last = gather_last(rows[0:8], rows[8:16], 8)
            blocks.append(jnp.concatenate([rows, last], 0).astype(BF16))
        products = dot_tn(jnp.concatenate(blocks, 1), table_ref[...])
        first_row = group * HALF * 4
        for block in range(2):
            re = products[block * 128 : block * 128 + HALF, :256]
            im = products[block * 128 + 64 : block * 128 + 64 + HALF, 256:]
            total = (re + im) * scale
            for part in range(2):
                start = first_row + block * 2 + part
                out_ref[pl.ds(start, HALF, stride=4), :] = total[:, part * 128 : part * 128 + 128]
        rows = pl.ds(first_row, HALF * 4)
        copies.append(pltpu.make_async_copy(out_ref.at[rows], out_hbm.at[rows], sem.at[group]))
        copies[-1].start()
    for copy in copies:
        copy.wait()


def vmem(count):
    return [pl.BlockSpec(memory_space=pltpu.VMEM)] * count


def grant(mib):
    return pltpu.CompilerParams(vmem_limit_bytes=mib * 2**20)


def local_call(kernel, name, result, scratch, *operands):
    return pl.pallas_call(
        kernel,
        out_shape=result,
        in_specs=vmem(len(operands)),
        out_specs=pl.BlockSpec(memory_space=pltpu.VMEM),
        scratch_shapes=[pltpu.VMEM(shape, F32) for shape in scratch],
        compiler_params=grant(8),
        name=name,
    )(*operands)


def chunks_of(*shape):
    return jax.ShapeDtypeStruct(shape, BF16)


def frequencies(spectrum, kernel):
    return pl.pallas_call(
        frequency_kernel,
        out_shape=jax.ShapeDtypeStruct((16, 4, 16, 128), BF16),
        in_specs=vmem(1) + [pl.BlockSpec(memory_space=pltpu.HBM)],
        out_specs=pl.BlockSpec(memory_space=pltpu.VMEM),
        scratch_shapes=[
            pltpu.VMEM((1216, 256), BF16),
            pltpu.VMEM((KZ, 2, 76, 16, 152), BF16),
            pltpu.VMEM((KZ, 64, 512), BF16),
            pltpu.VMEM((KZ, 64, 1216), BF16),
            pltpu.VMEM((3072, 128), F32),
            pltpu.VMEM((ROWS, 960, 128), F32),
            pltpu.SemaphoreType.DMA((KZ,)),
        ],
        compiler_params=grant(40),
        name="frequencies",
    )(spectrum, kernel)


def from_z(data, table, scale):
    return pl.pallas_call(
        functools.partial(from_z_kernel, scale),
        out_shape=jax.ShapeDtypeStruct((608, 128), F32),
        in_specs=vmem(2),
        out_specs=pl.BlockSpec(memory_space=pltpu.HBM),
        scratch_shapes=[pltpu.VMEM((608, 128), F32), pltpu.SemaphoreType.DMA((4,))],
        compiler_params=grant(8),
        name="from_z",
    )(data, table)


def exchange(chunks, axes):
    return lax.all_to_all(chunks, axes, 0, 0, tiled=True)


def on_device(multipoles, kernel):
    near = ("bx", "by")
    plane = (1024, 128)
    field = multipoles[:, :, 0, :].transpose(1, 0, 2)
    rows = local_call(
        spread_rows_kernel, "spread_rows", chunks_of(64, 16, 128), [(4, 168, 128), (1344, 128)], field
    )
    rows = exchange(rows, near)
    spectrum = local_call(
        to_waves_kernel, "to_waves", chunks_of(64, 2, 16, 128), [plane, plane, plane], rows
    )
    spectrum = exchange(spectrum.reshape(128, 16, 128), ("bx", "by", "col"))
    local = frequencies(spectrum, kernel.transpose(0, 1, 3, 4, 2, 5))
    local = exchange(local.reshape(64, 16, 128), near)
    back = local_call(
        from_waves_kernel, "from_waves", chunks_of(64, 1, 16, 128), [plane, plane], local
    )
    back = exchange(back.reshape(64, 16, 128), near)
    behind = jnp.asarray(table_back())
    result = from_z(back.reshape(16, 4, 16, 128), behind, 1.0 / (32 * SCALE))
    return result.reshape(multipoles.shape)


def solution(mesh):
    placed = (P(None, "col", "bx", "by"), P(None, "bx", "by", None, "col", None))
    return jax.shard_map(
        on_device, mesh=mesh, in_specs=placed, out_specs=P(None, "col", "bx", "by"), check_vma=False
    )
```
